32 devices in a mesh: blk: 8 (over y, x, core), tm: 4 (over z).
Axes of the slice: x: 2, y: 2, z: 4, core: 2. Of those that a mesh axis runs over, the one named last changes fastest.
Arguments:
- records: float32 [1024, 32768], P('blk', 'tm'), may hold values from -420 to 420
- gaps: int32 [2, 8, 8], P(None, 'blk', 'tm'), may hold values from 0 to 4096, as said below
Outputs:
- correlation: float32 [1024, 8, 4096], P(('blk', 'tm'))
The draws below stay inside these ranges and needn't reach their ends.
Inputs may be any that keep to these rules, and one draw needn't show every extreme that they name: For every window, gaps[0] + gaps[1] <= 4096; a window either has no valid sample or at least 1024 of them. Among the 2 windows of one channel block on one index of tm, exactly one has valid samples.
All inputs are finite; a program needn't handle non-finite values.
Results may differ from the reference program's by a relative error of at most 0.0003.
Values sent between devices are 32-bit elements; how exact they have to be, the bound alone decides.
No kernel may reach another device: no remote copies, remote signals or barrier semaphores. Data moves between devices by JAX's collectives and lax.ppermute only.
A program may use at most 256 MiB of HBM per device.

```python
import math
import jax
import jax.numpy as jnp
from jax import lax

NFFT = 4096
BAND = 64
CH_DEV = 128
WIN_DEV = 2
LIVE_DEV = 1
NBIN = 2048
NWIN = 8
NCH = 1024
N_BLK = 8
N_TM = 4


def draw_records(key, part):
    keys = jax.random.split(key, 5)
    total = NWIN * NFFT
    noise = jax.random.truncated_normal(keys[0], -6.0, 6.0, (NCH, total), jnp.float32)
    gains = jnp.exp(jax.random.uniform(keys[1], (NCH, 1), jnp.float32, 0.0, math.log(10.0)))
    amps = jax.random.uniform(keys[2], (NCH, 2), jnp.float32, 1.0, 4.0)
    bins = jax.random.randint(keys[3], (NCH, 2), 1, NBIN)
    offsets = jax.random.uniform(keys[4], (NCH, 2), jnp.float32, -math.pi, math.pi)
    spots = jnp.arange(NFFT)
    first = bins[:, 0:1] * spots[None, :] % NFFT
    second = bins[:, 1:2] * spots[None, :] % NFFT
    tones = amps[:, 0:1] * jnp.cos(2.0 * math.pi / NFFT * first.astype(jnp.float32) + offsets[:, 0:1])
    tones = tones + amps[:, 1:2] * jnp.cos(2.0 * math.pi / NFFT * second.astype(jnp.float32) + offsets[:, 1:2])
    signal = noise.reshape(NCH, NWIN, NFFT) + tones[:, None, :]
    return (signal.reshape(NCH, total) * gains).astype(jnp.float32)


def draw_gaps(key, part):
    keys = jax.random.split(key, 5)
    groups = N_BLK * N_TM
    ranks = jax.vmap(lambda k: jax.random.permutation(k, WIN_DEV))(jax.random.split(keys[0], groups))
    ranks = ranks.reshape(N_BLK, N_TM, WIN_DEV)
    live = jax.random.randint(keys[1], (N_BLK, N_TM, 1), 1, LIVE_DEV + 1)
    chosen = jax.random.randint(keys[2], (), 0, groups)
    flat = jnp.arange(groups).reshape(N_BLK, N_TM, 1)
    live = jnp.where(flat == chosen, LIVE_DEV, live)
    counts = jax.random.randint(keys[3], (N_BLK, N_TM, WIN_DEV), NFFT // 4, NFFT)
    full = (flat == chosen) & (ranks == 0)
    counts = jnp.where(full, NFFT, counts)
    counts = jnp.where(ranks < live, counts, 0)
    starts = jax.random.randint(keys[4], (N_BLK, N_TM, WIN_DEV), 0, NFFT + 1)
    starts = starts % (NFFT - counts + 1)
    stacked = jnp.stack([starts, counts], axis=0)
    return stacked.reshape(2, N_BLK, N_TM * WIN_DEV).astype(jnp.int32)


def setup_inputs(seed: int = 0) -> dict:
    key_of = jax.random.split(jax.random.key(seed), 3)
    return {
        "records": draw_records(jax.random.fold_in(key_of[2], 71), 0),
        "gaps": draw_gaps(jax.random.fold_in(key_of[2], 71), 0),
    }


EPS = 1e-05

def reference(records, gaps):
    spots = jnp.arange(NFFT)
    taper = 0.5 - 0.5 * jnp.cos(2.0 * math.pi / NFFT * spots.astype(jnp.float32))
    highest = lax.Precision.HIGHEST

    def block(args):
        rows, starts, counts = args
        frames = rows.reshape(CH_DEV, NWIN, NFFT)
        keep = (spots[None, :] >= starts[:, None]) & (spots[None, :] < (starts + counts)[:, None])
        tapered = jnp.where(keep[None], frames, 0.0) * taper
        spectrum = jnp.fft.rfft(tapered, axis=-1)[..., :NBIN]
        real_part = jnp.real(spectrum)
        imag_part = jnp.imag(spectrum)
        power = lax.optimization_barrier(jnp.mean((real_part * real_part + imag_part * imag_part).reshape(CH_DEV, NWIN, NBIN // BAND, BAND), axis=-1))
        scale = jnp.repeat(1.0 / jnp.sqrt(power + EPS), BAND, axis=-1)
        return (real_part * scale, imag_part * scale)
    white_re, white_im = lax.map(block, (records.reshape(N_BLK, CH_DEV, NWIN * NFFT), gaps[0], gaps[1]))
    white_re = white_re.reshape(NCH, NWIN, NBIN)
    white_im = white_im.reshape(NCH, NWIN, NBIN)
    source_re = white_re[::CH_DEV]
    source_im = white_im[::CH_DEV]
    norm = 1.0 / math.sqrt(NFFT * NWIN)

    def one(pair):
        s_re, s_im = pair
        cross_re = jnp.einsum('cwk,wk->ck', white_re, s_re, precision=highest) + jnp.einsum('cwk,wk->ck', white_im, s_im, precision=highest)
        cross_im = jnp.einsum('cwk,wk->ck', white_im, s_re, precision=highest) - jnp.einsum('cwk,wk->ck', white_re, s_im, precision=highest)
        cross = lax.complex(cross_re, cross_im)
        full = jnp.concatenate([cross, jnp.zeros_like(cross[:, :1])], axis=1)
        lagged = jnp.fft.irfft(full, n=NFFT, axis=-1) * NFFT
        return jnp.roll(lagged, NBIN, axis=-1) * norm
    stacked = lax.map(one, (source_re, source_im))
    return jnp.transpose(stacked, (1, 0, 2))
```

```python
import functools
import math

import jax
import jax.numpy as jnp
import numpy as np
from jax import lax
from jax.experimental import pallas as pl
from jax.experimental.pallas import tpu as pltpu
from jax.sharding import PartitionSpec as P

NFFT = 4096
BAND = 64
EPS = 1e-05
LANES = 128
SUB = 8
RADIX = NFFT // LANES
HALF = RADIX // 2
ROWS = HALF + 1
QUART = LANES // 2
PAD = ROWS * SUB


def split_bf16(table):
    high = table.astype(jnp.bfloat16)
    low = (table - high.astype(np.float32)).astype(jnp.bfloat16)
    return high, low


def bin_order():
    half = np.arange(QUART // 2)
    return np.concatenate([2 * half, 2 * half + 1])


def dft_tables():
    spots = np.arange(LANES)[:, None]
    order = bin_order()[None, :]
    direct = 2.0 * np.pi / LANES * (spots * order % LANES)
    mirror = 2.0 * np.pi / LANES * (spots * (LANES - 1 - order) % LANES)
    upper = np.concatenate([np.cos(direct), np.cos(mirror), -np.sin(direct), np.sin(mirror)], 1)
    lower = np.concatenate([np.sin(direct), np.sin(mirror), np.cos(direct), -np.cos(mirror)], 1)
    full = np.concatenate([upper, lower], 0).astype(np.float32)
    tables = []
    for one in (full, full.T):
        high, low = split_bf16(one)
        tables.append(np.concatenate([high, high, low], 0))
    return tables


def twist_table():
    rows = np.arange(ROWS)[:, None]
    angle = 2.0 * np.pi / NFFT * (rows * np.arange(LANES)[None, :])
    return np.concatenate([np.cos(angle), np.sin(angle)], 0).astype(np.float32)


def bin_weights(norm):
    rows = np.arange(HALF)[:, None]
    order = bin_order()[None, :]
    direct = rows + RADIX * order
    mirror = np.where(rows == 0, HALF, RADIX - rows) + RADIX * order
    bins = np.concatenate([direct, mirror], 1)
    return (np.where(bins == 0, 1.0, 2.0) * np.where(bins % 2 == 0, 1.0, -1.0) * norm).astype(np.float32)


def turn(re, im, c, s):
    if abs(c - s) < 1e-12:
        return (re + im) * c, (im - re) * c
    if abs(c + s) < 1e-12:
        return (im - re) * s, -(re + im) * s
    return re * c + im * s, im * c - re * s


def real_fft(x):
    n = len(x)
    if n == 2:
        return [x[0] + x[1], x[0] - x[1]], [None, None]
    er, ei = real_fft(x[0::2])
    odr, odi = real_fft(x[1::2])
    half, quarter = n // 2, n // 4
    re, im = [None] * (half + 1), [None] * (half + 1)
    re[0], re[half] = er[0] + odr[0], er[0] - odr[0]
    re[quarter], im[quarter] = er[quarter], -odr[quarter]
    for k in range(1, quarter):
        angle = 2.0 * math.pi * k / n
        tr, ti = turn(odr[k], odi[k], math.cos(angle), math.sin(angle))
        re[k], im[k] = er[k] + tr, ei[k] + ti
        re[half - k], im[half - k] = er[k] - tr, ti - ei[k]
    return re, im


def real_fft_adjoint(re, im):
    half = len(re) - 1
    n = 2 * half
    if n == 2:
        return [re[0] + re[1], re[0] - re[1]]
    quarter = n // 4
    er, ei = [None] * (quarter + 1), [None] * (quarter + 1)
    odr, odi = [None] * (quarter + 1), [None] * (quarter + 1)
    er[0], odr[0] = re[0] + re[half], re[0] - re[half]
    er[quarter], odr[quarter] = re[quarter], -im[quarter]
    for k in range(1, quarter):
        er[k], ei[k] = re[k] + re[half - k], im[k] - im[half - k]
        tr, ti = re[k] - re[half - k], im[k] + im[half - k]
        angle = 2.0 * math.pi * k / n
        odr[k], odi[k] = turn(tr, ti, math.cos(angle), -math.sin(angle))
    even = real_fft_adjoint(er, ei)
    odd = real_fft_adjoint(odr, odi)
    out = [None] * n
    out[0::2] = even
    out[1::2] = odd
    return out


def matmul(rows, table):
    high = rows.astype(jnp.bfloat16)
    low = (rows - high.astype(jnp.float32)).astype(jnp.bfloat16)
    wide = jnp.concatenate([high, low, high], axis=1)
    return jnp.dot(wide, table, preferred_element_type=jnp.float32)


def lane_ids():
    return lax.broadcasted_iota(jnp.int32, (SUB, LANES), 1)


def lift(x, twist_ref, grid_ref, base):
    re, im = real_fft(x)
    for k in range(ROWS):
        if k == 0:
            zr, zi = re[0], jnp.zeros_like(re[0])
        else:
            c = twist_ref[k : k + 1, :]
            s = twist_ref[ROWS + k : ROWS + k + 1, :]
            if k == HALF:
                zr, zi = re[k] * c, -(re[k] * s)
            else:
                zr, zi = re[k] * c + im[k] * s, im[k] * c - re[k] * s
        spot = pl.ds(base + k * SUB, SUB)
        grid_ref[spot, :LANES] = zr
        grid_ref[spot, LANES:] = zi


def whiten(spec_ref, base):
    first = lane_ids() < QUART
    re, im = [], []
    for k in range(HALF):
        spot = pl.ds(base + k * SUB, SUB)
        r, i = spec_ref[spot, :LANES], spec_ref[spot, LANES:]
        if k == 0:
            last = pl.ds(base + HALF * SUB, SUB)
            r = jnp.where(first, r, spec_ref[last, :LANES])
            i = jnp.where(first, i, spec_ref[last, LANES:])
        re.append(r)
        im.append(i)
    power = re[0] * re[0] + im[0] * im[0]
    for r, i in zip(re[1:], im[1:]):
        power = power + (r * r + i * i)
    power = power + pltpu.roll(power, QUART, 1)
    power = power + pltpu.roll(power, QUART // 2, 1)
    scale = 1.0 / jnp.sqrt(power * (1.0 / BAND) + EPS)
    return [r * scale for r in re], [i * scale for i in im]


def source_kernel(windows, group, me_ref, raw_ref, twist_ref, table_ref, weight_ref, out_ref, grid_ref):
    sources = raw_ref.shape[0] // (windows * RADIX)
    lanes = lane_ids()
    me = me_ref[0]
    span = windows * RADIX
    for w in range(windows):
        own = jnp.broadcast_to(raw_ref[pl.ds(me * span + w * RADIX, 1), :1], (SUB, 1))
        for g in range(sources // group):
            x = [raw_ref[pl.ds(g * group * span + w * RADIX + v, SUB, stride=span), :] for v in range(RADIX)]
            match = jnp.where(x[0][:, :1] == own, 1.0, 0.0)
            x[0] = jnp.where(lanes == 0, 0.0, x[0])
            lift(x, twist_ref, grid_ref, 0)
            grid_ref[...] = matmul(grid_ref[...], table_ref[...])
            re, im = whiten(grid_ref, 0)
            for k in range(HALF):
                weight = weight_ref[k : k + 1, :] * match
                spot = pl.ds((w * HALF + k) * sources + g * group, SUB)
                out_ref[spot, :LANES] = re[k] * weight
                out_ref[spot, LANES:] = im[k] * weight


def main_kernel(windows, batch, *refs):
    ins, (source_ref, twist_ref, table_ref, back_ref, out_ref, grid_ref, spec_ref, cross_ref) = refs[:windows], refs[windows:]
    group = pl.program_id(1)
    sources = source_ref.shape[0] // (windows * HALF)
    first = lane_ids() < QUART

    @pl.when(group == 0)
    def _():
        for w in range(windows):
            x = [ins[w][:, v * LANES : (v + 1) * LANES] for v in range(RADIX)]
            lift(x, twist_ref, grid_ref, w * PAD)
        grid_ref[...] = matmul(grid_ref[...], table_ref[...])
        for w in range(windows):
            re, im = whiten(grid_ref, w * PAD)
            for k in range(HALF):
                spec_ref[:, w * HALF + k, :LANES] = re[k]
                spec_ref[:, w * HALF + k, LANES:] = im[k]

    def some(step, _):
        start = step * batch

        def combine(k):
            found = []
            parts = []
            for w in range(windows):
                spot = pl.ds((w * HALF + k) * sources + group * SUB, SUB)
                parts.append((source_ref[spot, :LANES], source_ref[spot, LANES:]))
            for c in range(batch):
                re = im = None
                for w in range(windows):
                    ur, ui = parts[w]
                    row = w * HALF + k
                    sr = spec_ref[start + c, row : row + 1, :LANES]
                    si = spec_ref[start + c, row : row + 1, LANES:]
                    r, i = sr * ur + si * ui, si * ur - sr * ui
                    re, im = (r, i) if re is None else (re + r, im + i)
                found.append((re, im))
            return found

        for c, (re, im) in enumerate(combine(0)):
            cross_ref[pl.ds(c * PAD, SUB), :LANES] = jnp.where(first, re, 0.0)
            cross_ref[pl.ds(c * PAD, SUB), LANES:] = jnp.where(first, im, 0.0)
            cross_ref[pl.ds(c * PAD + HALF * SUB, SUB), :LANES] = jnp.where(first, 0.0, re)
            cross_ref[pl.ds(c * PAD + HALF * SUB, SUB), LANES:] = jnp.where(first, 0.0, im)
        for k in range(1, HALF):
            for c, (re, im) in enumerate(combine(k)):
                spot = pl.ds(c * PAD + k * SUB, SUB)
                cross_ref[spot, :LANES] = re
                cross_ref[spot, LANES:] = im
        cross_ref[...] = matmul(cross_ref[...], back_ref[...])
        for c in range(batch):
            re, im = [], []
            for k in range(ROWS):
                spot = pl.ds(c * PAD + k * SUB, SUB)
                r, i = cross_ref[spot, :LANES], cross_ref[spot, LANES:]
                if k == 0:
                    i = None
                else:
                    cos = twist_ref[k : k + 1, :]
                    sin = twist_ref[ROWS + k : ROWS + k + 1, :]
                    r, i = r * cos - i * sin, (None if k == HALF else i * cos + r * sin)
                re.append(r)
                im.append(i)
            lags = real_fft_adjoint(re, im)
            for v in range(RADIX):
                out_ref[start + c, :, v * LANES : (v + 1) * LANES] = lags[v]
        return 0

    lax.fori_loop(0, SUB // batch, some, 0)


def resident(array):
    return pl.BlockSpec(array.shape, lambda *_: (0,) * array.ndim)


def source_spectra(raw, me, windows, tables):
    twist, forward, _, weights = tables
    sources = raw.shape[0] // (windows * RADIX)
    group = SUB
    shape = (windows * HALF * sources, 2 * LANES)
    return pl.pallas_call(
        functools.partial(source_kernel, windows, group),
        out_shape=jax.ShapeDtypeStruct(shape, jnp.float32),
        grid_spec=pltpu.PrefetchScalarGridSpec(
            num_scalar_prefetch=1,
            grid=(1,),
            in_specs=[resident(raw), resident(twist), resident(forward), resident(weights)],
            out_specs=pl.BlockSpec(shape, lambda *_: (0, 0)),
            scratch_shapes=[pltpu.VMEM((PAD, 2 * LANES), jnp.float32)],
        ),
        name="sources",
    )(me.reshape(1), raw, twist, forward, weights)


def correlations(pieces, source, tables, total, first, before, batch=4):
    twist, forward, back, _ = tables
    windows = len(pieces)
    sources = source.shape[0] // (windows * HALF)
    rows = pieces[0].shape[0]
    offset = first // SUB
    args = [*pieces, source, twist, forward, back]
    specs = [pl.BlockSpec((SUB, NFFT), lambda c, g: (c, 0))] * windows
    specs += [resident(a) for a in args[windows:]]
    aliases = {}
    if before is not None:
        aliases = {len(args): 0}
        args.append(before)
        specs.append(pl.BlockSpec(memory_space=pl.ANY))

    def body(*refs):
        if before is not None:
            refs = refs[: windows + 4] + refs[windows + 5 :]
        main_kernel(windows, batch, *refs)

    return pl.pallas_call(
        body,
        out_shape=jax.ShapeDtypeStruct((total, sources, NFFT), jnp.float32),
        grid=(rows // SUB, sources // SUB),
        in_specs=specs,
        out_specs=pl.BlockSpec((SUB, SUB, NFFT), lambda c, g: (c + offset, g, 0)),
        scratch_shapes=[
            pltpu.VMEM((windows * PAD, 2 * LANES), jnp.float32),
            pltpu.VMEM((SUB, windows * HALF, 2 * LANES), jnp.float32),
            pltpu.VMEM((batch * PAD, 2 * LANES), jnp.float32),
        ],
        input_output_aliases=aliases,
        compiler_params=pltpu.CompilerParams(vmem_limit_bytes=40 * 2**20),
        name=f"lags_{first}",
    )(*args)


def shards(records, gaps):
    width = records.shape[0]
    slots = records.shape[1] // NFFT
    windows = lax.axis_size("tm")
    here = lax.axis_index("tm")
    mine = width // windows
    starts, counts = gaps[0, 0], gaps[1, 0]
    live = jnp.argmax(counts).astype(jnp.int32)
    start, count = starts[live], counts[live]
    spots = np.arange(NFFT)
    taper = jnp.asarray((0.5 - 0.5 * np.cos(2.0 * np.pi / NFFT * spots)).astype(np.float32))
    taper = jnp.where((spots >= start) & (spots < start + count), taper, 0.0)
    frames = lax.dynamic_slice(records, (jnp.int32(0), live * NFFT), (width, NFFT))
    tapered = jnp.where(taper == 0.0, 0.0, frames) * taper
    parted = tapered.reshape(windows, mine, NFFT)

    def shift(array, step):
        pairs = [(i, (i + step) % windows) for i in range(windows)]
        return lax.ppermute(array, "tm", pairs)

    def part(step):
        return lax.dynamic_index_in_dim(parted, (here + step) % windows, 0, keepdims=False)

    last = SUB
    cut = mine - last
    steps = list(range(1, windows))
    own = part(0)
    head = [own[:cut]] + [shift(part(d)[:cut], d) for d in steps]
    tail = [own[cut:]] + [shift(part(d)[cut:], d) for d in steps]

    row = jnp.where(spots == 0, live.astype(jnp.float32), tapered[0]).reshape(RADIX, LANES)
    rows = jnp.stack([row] + [shift(row, d) for d in steps])
    raw = lax.all_gather(rows, "blk", axis=0, tiled=False)
    raw = raw.reshape(-1, LANES)

    norm = 1.0 / math.sqrt(NFFT * slots * windows)
    forward, back = dft_tables()
    tables = (jnp.asarray(twist_table()), jnp.asarray(forward), jnp.asarray(back), jnp.asarray(bin_weights(norm)))
    source = source_spectra(raw, lax.axis_index("blk").astype(jnp.int32), windows, tables)
    out = correlations(head, source, tables, mine, 0, None)
    return correlations(tail, source, tables, mine, cut, out)


def solution(mesh):
    in_specs = (P("blk", "tm"), P(None, "blk", "tm"))
    out_specs = P(("blk", "tm"), None, None)
    return jax.shard_map(shards, mesh=mesh, in_specs=in_specs, out_specs=out_specs, check_vma=False)
```

```python
import functools
import math

import jax
import jax.numpy as jnp
import numpy as np
from jax import lax
from jax.experimental import pallas as pl
from jax.experimental.pallas import tpu as pltpu
from jax.sharding import PartitionSpec as P

NFFT = 4096
BAND = 64
EPS = 1e-05
LANES = 128
SUB = 8
RADIX = NFFT // LANES
HALF = RADIX // 2
ROWS = HALF + 1
QUART = LANES // 2
PAD = ROWS * SUB


def split_bf16(table):
    high = table.astype(jnp.bfloat16)
    low = (table - high.astype(np.float32)).astype(jnp.bfloat16)
    return high, low


def bin_order():
    half = np.arange(QUART // 2)
    return np.concatenate([2 * half, 2 * half + 1])


def dft_tables():
    spots = np.arange(LANES)[:, None]
    order = bin_order()[None, :]
    direct = 2.0 * np.pi / LANES * (spots * order % LANES)
    mirror = 2.0 * np.pi / LANES * (spots * (LANES - 1 - order) % LANES)
    upper = np.concatenate([np.cos(direct), np.cos(mirror), -np.sin(direct), np.sin(mirror)], 1)
    lower = np.concatenate([np.sin(direct), np.sin(mirror), np.cos(direct), -np.cos(mirror)], 1)
    full = np.concatenate([upper, lower], 0).astype(np.float32)
    tables = []
    for one in (full, full.T):
        high, low = split_bf16(one)
        tables.append(np.concatenate([high, high, low], 0))
    return tables


def twist_table():
    rows = np.arange(ROWS)[:, None]
    angle = 2.0 * np.pi / NFFT * (rows * np.arange(LANES)[None, :])
    return np.concatenate([np.cos(angle), np.sin(angle)], 0).astype(np.float32)


def bin_weights(norm):
    rows = np.arange(HALF)[:, None]
    order = bin_order()[None, :]
    direct = rows + RADIX * order
    mirror = np.where(rows == 0, HALF, RADIX - rows) + RADIX * order
    bins = np.concatenate([direct, mirror], 1)
    return (np.where(bins == 0, 1.0, 2.0) * np.where(bins % 2 == 0, 1.0, -1.0) * norm).astype(np.float32)


def turn(re, im, c, s):
    if abs(c - s) < 1e-12:
        return (re + im) * c, (im - re) * c
    if abs(c + s) < 1e-12:
        return (im - re) * s, -(re + im) * s
    return re * c + im * s, im * c - re * s


def real_fft(x):
    n = len(x)
    if n == 2:
        return [x[0] + x[1], x[0] - x[1]], [None, None]
    er, ei = real_fft(x[0::2])
    odr, odi = real_fft(x[1::2])
    half, quarter = n // 2, n // 4
    re, im = [None] * (half + 1), [None] * (half + 1)
    re[0], re[half] = er[0] + odr[0], er[0] - odr[0]
    re[quarter], im[quarter] = er[quarter], -odr[quarter]
    for k in range(1, quarter):
        angle = 2.0 * math.pi * k / n
        tr, ti = turn(odr[k], odi[k], math.cos(angle), math.sin(angle))
        re[k], im[k] = er[k] + tr, ei[k] + ti
        re[half - k], im[half - k] = er[k] - tr, ti - ei[k]
    return re, im


def real_fft_adjoint(re, im):
    half = len(re) - 1
    n = 2 * half
    if n == 2:
        return [re[0] + re[1], re[0] - re[1]]
    quarter = n // 4
    er, ei = [None] * (quarter + 1), [None] * (quarter + 1)
    odr, odi = [None] * (quarter + 1), [None] * (quarter + 1)
    er[0], odr[0] = re[0] + re[half], re[0] - re[half]
    er[quarter], odr[quarter] = re[quarter], -im[quarter]
    for k in range(1, quarter):
        er[k], ei[k] = re[k] + re[half - k], im[k] - im[half - k]
        tr, ti = re[k] - re[half - k], im[k] + im[half - k]
        angle = 2.0 * math.pi * k / n
        odr[k], odi[k] = turn(tr, ti, math.cos(angle), -math.sin(angle))
    even = real_fft_adjoint(er, ei)
    odd = real_fft_adjoint(odr, odi)
    out = [None] * n
    out[0::2] = even
    out[1::2] = odd
    return out


def matmul(rows, table):
    high = rows.astype(jnp.bfloat16)
    low = (rows - high.astype(jnp.float32)).astype(jnp.bfloat16)
    wide = jnp.concatenate([high, low, high], axis=1)
    return jnp.dot(wide, table, preferred_element_type=jnp.float32)


def lane_ids():
    return lax.broadcasted_iota(jnp.int32, (SUB, LANES), 1)


def lift(x, twist_ref, grid_ref, base):
    re, im = real_fft(x)
    for k in range(ROWS):
        if k == 0:
            zr, zi = re[0], jnp.zeros_like(re[0])
        else:
            c = twist_ref[k : k + 1, :]
            s = twist_ref[ROWS + k : ROWS + k + 1, :]
            if k == HALF:
                zr, zi = re[k] * c, -(re[k] * s)
            else:
                zr, zi = re[k] * c + im[k] * s, im[k] * c - re[k] * s
        spot = pl.ds(base + k * SUB, SUB)
        grid_ref[spot, :LANES] = zr
        grid_ref[spot, LANES:] = zi


def whiten(spec_ref, base):
    first = lane_ids() < QUART
    re, im = [], []
    for k in range(HALF):
        spot = pl.ds(base + k * SUB, SUB)
        r, i = spec_ref[spot, :LANES], spec_ref[spot, LANES:]
        if k == 0:
            last = pl.ds(base + HALF * SUB, SUB)
            r = jnp.where(first, r, spec_ref[last, :LANES])
            i = jnp.where(first, i, spec_ref[last, LANES:])
        re.append(r)
        im.append(i)
    power = re[0] * re[0] + im[0] * im[0]
    for r, i in zip(re[1:], im[1:]):
        power = power + (r * r + i * i)
    power = power + pltpu.roll(power, QUART, 1)
    power = power + pltpu.roll(power, QUART // 2, 1)
    scale = 1.0 / jnp.sqrt(power * (1.0 / BAND) + EPS)
    return [r * scale for r in re], [i * scale for i in im]


def source_kernel(windows, group, me_ref, raw_ref, twist_ref, table_ref, weight_ref, out_ref, grid_ref):
    sources = raw_ref.shape[0] // (windows * RADIX)
    lanes = lane_ids()
    me = me_ref[0]
    span = windows * RADIX
    for w in range(windows):
        own = jnp.broadcast_to(raw_ref[pl.ds(me * span + w * RADIX, 1), :1], (SUB, 1))
        for g in range(sources // group):
            x = [raw_ref[pl.ds(g * group * span + w * RADIX + v, SUB, stride=span), :] for v in range(RADIX)]
            match = jnp.where(x[0][:, :1] == own, 1.0, 0.0)
            x[0] = jnp.where(lanes == 0, 0.0, x[0])
            lift(x, twist_ref, grid_ref, 0)
            grid_ref[...] = matmul(grid_ref[...], table_ref[...])
            re, im = whiten(grid_ref, 0)
            for k in range(HALF):
                weight = weight_ref[k : k + 1, :] * match
                spot = pl.ds((w * HALF + k) * sources + g * group, SUB)
                out_ref[spot, :LANES] = re[k] * weight
                out_ref[spot, LANES:] = im[k] * weight


def main_kernel(windows, batch, split, *refs):
    ins, refs = refs[:windows], refs[windows:]
    extra, refs = (refs[0], refs[1:]) if split is not None else (None, refs)
    source_ref, twist_ref, table_ref, back_ref, out_ref, grid_ref, spec_ref, cross_ref = refs
    group = pl.program_id(1)
    sources = source_ref.shape[0] // (windows * HALF)
    first = lane_ids() < QUART

    @pl.when(group == 0)
    def _():
        for w in range(windows):
            x = [ins[w][:, v * LANES : (v + 1) * LANES] for v in range(RADIX)]
            if w == split:
                lead = pl.program_id(0) == 0
                x = [jnp.where(lead, extra[1:, v, :], x[v]) for v in range(RADIX)]
            lift(x, twist_ref, grid_ref, w * PAD)
        grid_ref[...] = matmul(grid_ref[...], table_ref[...])
        for w in range(windows):
            re, im = whiten(grid_ref, w * PAD)
            for k in range(HALF):
                spec_ref[:, w * HALF + k, :LANES] = re[k]
                spec_ref[:, w * HALF + k, LANES:] = im[k]

    def some(step, _):
        start = step * batch

        def combine(k):
            found = []
            parts = []
            for w in range(windows):
                spot = pl.ds((w * HALF + k) * sources + group * SUB, SUB)
                parts.append((source_ref[spot, :LANES], source_ref[spot, LANES:]))
            for c in range(batch):
                re = im = None
                for w in range(windows):
                    ur, ui = parts[w]
                    row = w * HALF + k
                    sr = spec_ref[start + c, row : row + 1, :LANES]
                    si = spec_ref[start + c, row : row + 1, LANES:]
                    r, i = sr * ur + si * ui, si * ur - sr * ui
                    re, im = (r, i) if re is None else (re + r, im + i)
                found.append((re, im))
            return found

        for c, (re, im) in enumerate(combine(0)):
            cross_ref[pl.ds(c * PAD, SUB), :LANES] = jnp.where(first, re, 0.0)
            cross_ref[pl.ds(c * PAD, SUB), LANES:] = jnp.where(first, im, 0.0)
            cross_ref[pl.ds(c * PAD + HALF * SUB, SUB), :LANES] = jnp.where(first, 0.0, re)
            cross_ref[pl.ds(c * PAD + HALF * SUB, SUB), LANES:] = jnp.where(first, 0.0, im)
        for k in range(1, HALF):
            for c, (re, im) in enumerate(combine(k)):
                spot = pl.ds(c * PAD + k * SUB, SUB)
                cross_ref[spot, :LANES] = re
                cross_ref[spot, LANES:] = im
        cross_ref[...] = matmul(cross_ref[...], back_ref[...])
        for c in range(batch):
            re, im = [], []
            for k in range(ROWS):
                spot = pl.ds(c * PAD + k * SUB, SUB)
                r, i = cross_ref[spot, :LANES], cross_ref[spot, LANES:]
                if k == 0:
                    i = None
                else:
                    cos = twist_ref[k : k + 1, :]
                    sin = twist_ref[ROWS + k : ROWS + k + 1, :]
                    r, i = r * cos - i * sin, (None if k == HALF else i * cos + r * sin)
                re.append(r)
                im.append(i)
            lags = real_fft_adjoint(re, im)
            for v in range(RADIX):
                out_ref[start + c, :, v * LANES : (v + 1) * LANES] = lags[v]
        return 0

    lax.fori_loop(0, SUB // batch, some, 0)


def resident(array):
    return pl.BlockSpec(array.shape, lambda *_: (0,) * array.ndim)


def source_spectra(raw, me, windows, tables):
    twist, forward, _, weights = tables
    sources = raw.shape[0] // (windows * RADIX)
    group = SUB
    shape = (windows * HALF * sources, 2 * LANES)
    return pl.pallas_call(
        functools.partial(source_kernel, windows, group),
        out_shape=jax.ShapeDtypeStruct(shape, jnp.float32),
        grid_spec=pltpu.PrefetchScalarGridSpec(
            num_scalar_prefetch=1,
            grid=(1,),
            in_specs=[resident(raw), resident(twist), resident(forward), resident(weights)],
            out_specs=pl.BlockSpec(shape, lambda *_: (0, 0)),
            scratch_shapes=[pltpu.VMEM((PAD, 2 * LANES), jnp.float32)],
        ),
        name="sources",
    )(me.reshape(1), raw, twist, forward, weights)


def correlations(pieces, starts, lead, source, tables, total, first, rows, before, batch=4):
    twist, forward, back, _ = tables
    windows = len(pieces)
    sources = source.shape[0] // (windows * HALF)
    offset = first // SUB
    args = list(pieces)
    shifts = [(first - s) // SUB for s in starts]
    specs = [pl.BlockSpec((SUB, NFFT), lambda c, g, n=n: (jnp.maximum(c + n, 0), 0)) for n in shifts]
    split = None
    if lead is not None:
        split = starts.index(SUB)
        args.append(lead)
        specs.append(resident(lead))
    fixed = [source, twist, forward, back]
    args += fixed
    specs += [resident(a) for a in fixed]
    inputs = len(args)
    aliases = {}
    if before is not None:
        aliases = {inputs: 0}
        args.append(before)
        specs.append(pl.BlockSpec(memory_space=pl.ANY))

    def body(*refs):
        if before is not None:
            refs = refs[:inputs] + refs[inputs + 1 :]
        main_kernel(windows, batch, split, *refs)

    return pl.pallas_call(
        body,
        out_shape=jax.ShapeDtypeStruct((total, sources, NFFT), jnp.float32),
        grid=(rows // SUB, sources // SUB),
        in_specs=specs,
        out_specs=pl.BlockSpec((SUB, SUB, NFFT), lambda c, g: (c + offset, g, 0)),
        scratch_shapes=[
            pltpu.VMEM((windows * PAD, 2 * LANES), jnp.float32),
            pltpu.VMEM((SUB, windows * HALF, 2 * LANES), jnp.float32),
            pltpu.VMEM((batch * PAD, 2 * LANES), jnp.float32),
        ],
        input_output_aliases=aliases,
        compiler_params=pltpu.CompilerParams(vmem_limit_bytes=40 * 2**20),
        name=f"lags_{first}",
    )(*args)


def taper_kernel(parts, mine, windows, row, gaps_ref, taper_ref, records_ref, *refs):
    refs = refs if row else refs[1:]
    outs, sems = refs[2:3] if row else refs[: len(parts)], refs[-1]
    here = lax.axis_index("tm")
    live, most = jnp.int32(0), gaps_ref[1, 0, 0]
    for slot in range(1, gaps_ref.shape[2]):
        better = gaps_ref[1, 0, slot] > most
        live = jnp.where(better, slot, live)
        most = jnp.where(better, gaps_ref[1, 0, slot], most)
    start = gaps_ref[0, 0, live]
    column = pl.ds(pl.multiple_of(live * NFFT, NFFT), NFFT)
    copies = []
    for n, (step, first, rows) in enumerate(parts):
        base = pl.multiple_of(lax.rem(here + step, windows) * mine + first, SUB)
        copies.append(pltpu.make_async_copy(records_ref.at[pl.ds(base, rows), column], outs[n], sems.at[n]))
    if row:
        copies.append(pltpu.make_async_copy(records_ref.at[pl.ds(0, SUB), column], refs[-2], sems.at[len(parts)]))
    for copy in copies:
        copy.start()
    spots = lax.broadcasted_iota(jnp.int32, (1, NFFT), 1)
    taper = jnp.where((spots >= start) & (spots < start + most), taper_ref[...], 0.0)
    for n, (step, first, rows) in enumerate(parts):
        copies[n].wait()
        if row:
            for v in range(RADIX):
                column = slice(v * LANES, (v + 1) * LANES)
                refs[0][1:, v, :] = outs[n][:, column] * taper[:, column]
            continue
        for r in range(0, rows, SUB):
            outs[n][r : r + SUB, :] = outs[n][r : r + SUB, :] * taper
    if row:
        copies[-1].wait()
        line = jnp.where(spots == 0, live.astype(jnp.float32), refs[-2][:1, :] * taper)
        for v in range(RADIX):
            refs[0][0, v : v + 1, :] = line[:, v * LANES : (v + 1) * LANES]
            refs[1][v : v + 1, :] = line[:, v * LANES : (v + 1) * LANES]


def tapered(records, gaps, parts, mine, windows, after=None):
    row = after is None
    spots = np.arange(NFFT)
    taper = jnp.asarray((0.5 - 0.5 * np.cos(2.0 * np.pi / NFFT * spots)).astype(np.float32)[None])
    shapes = [(rows, NFFT) for _, _, rows in parts]
    scratch = [pltpu.SemaphoreType.DMA((len(parts) + row,))]
    if row:
        shapes = [(1 + SUB, RADIX, LANES), (RADIX, LANES)]
        scratch = [pltpu.VMEM((SUB, NFFT), jnp.float32)] * 2 + scratch
    return pl.pallas_call(
        functools.partial(taper_kernel, parts, mine, windows, row),
        out_shape=[jax.ShapeDtypeStruct(shape, jnp.float32) for shape in shapes],
        in_specs=[
            pl.BlockSpec(memory_space=pltpu.SMEM),
            pl.BlockSpec(memory_space=pltpu.VMEM),
            pl.BlockSpec(memory_space=pltpu.HBM),
        ]
        + [pl.BlockSpec(memory_space=pl.ANY)] * (not row),
        out_specs=[pl.BlockSpec(memory_space=pltpu.VMEM) for _ in shapes],
        scratch_shapes=scratch,
        compiler_params=pltpu.CompilerParams(vmem_limit_bytes=16 * 2**20),
        name="taper_row" if row else "taper",
    )(gaps, taper, pltpu.with_memory_space_constraint(records, pltpu.HBM), *([] if row else [after]))


def shards(records, gaps):
    width = records.shape[0]
    slots = records.shape[1] // NFFT
    windows = lax.axis_size("tm")
    mine = width // windows
    far = windows // 2

    def shift(array, step):
        pairs = [(i, (i + step) % windows) for i in range(windows)]
        return lax.ppermute(array, "tm", pairs)

    cut = mine - SUB
    steps = list(range(1, windows))
    near = [d for d in steps if d != far]
    lead, row = tapered(records, gaps, [(far, 0, SUB)], mine, windows)
    lead = shift(lead, far)
    lines = [row] + [lead[0] if d == far else shift(row, d) for d in steps]
    rows = jnp.stack(lines)

    parts = [(far, SUB, cut - SUB)] + [(d, 0, mine) for d in near] + [(far, cut, SUB), (0, 0, mine)]
    bulk = tapered(records, gaps, parts, mine, windows, row)
    rows, lead, bulk = lax.optimization_barrier((rows, lead, bulk))
    middle, *whole, last, own = bulk
    middle = shift(middle, far)
    whole = [shift(array, d) for array, d in zip(whole, near)]
    last = shift(last, far)
    raw = lax.all_gather(rows, "blk", axis=0, tiled=False)
    raw = raw.reshape(-1, LANES)
    head = [own] + whole[: far - 1] + [middle] + whole[far - 1 :]
    tail = [own] + whole[: far - 1] + [last] + whole[far - 1 :]

    norm = 1.0 / math.sqrt(NFFT * slots * windows)
    forward, back = dft_tables()
    tables = (jnp.asarray(twist_table()), jnp.asarray(forward), jnp.asarray(back), jnp.asarray(bin_weights(norm)))
    source = source_spectra(raw, lax.axis_index("blk").astype(jnp.int32), windows, tables)
    starts = [SUB if d == far else 0 for d in range(windows)]
    out = correlations(head, starts, lead, source, tables, mine, 0, cut, None)
    starts = [cut if d == far else 0 for d in range(windows)]
    return correlations(tail, starts, None, source, tables, mine, cut, SUB, out)


def solution(mesh):
    in_specs = (P("blk", "tm"), P(None, "blk", "tm"))
    out_specs = P(("blk", "tm"), None, None)
    return jax.shard_map(shards, mesh=mesh, in_specs=in_specs, out_specs=out_specs, check_vma=False)
```

```python
import functools
import math

import jax
import jax.numpy as jnp
import numpy as np
from jax import lax
from jax.experimental import pallas as pl
from jax.experimental.pallas import tpu as pltpu
from jax.sharding import PartitionSpec as P

NFFT = 4096
BAND = 64
EPS = 1e-05
LANES = 128
SUB = 8
RADIX = NFFT // LANES
HALF = RADIX // 2
ROWS = HALF + 1
QUART = LANES // 2
PAD = ROWS * SUB


def split_bf16(table):
    high = table.astype(jnp.bfloat16)
    low = (table - high.astype(np.float32)).astype(jnp.bfloat16)
    return high, low


def bin_order():
    half = np.arange(QUART // 2)
    return np.concatenate([2 * half, 2 * half + 1])


def dft_tables():
    spots = np.arange(LANES)[:, None]
    order = bin_order()[None, :]
    direct = 2.0 * np.pi / LANES * (spots * order % LANES)
    mirror = 2.0 * np.pi / LANES * (spots * (LANES - 1 - order) % LANES)
    upper = np.concatenate([np.cos(direct), np.cos(mirror), -np.sin(direct), np.sin(mirror)], 1)
    lower = np.concatenate([np.sin(direct), np.sin(mirror), np.cos(direct), -np.cos(mirror)], 1)
    full = np.concatenate([upper, lower], 0).astype(np.float32)
    tables = []
    for one in (full, full.T):
        high, low = split_bf16(one)
        tables.append(np.concatenate([high, high, low], 0))
    return tables


def twist_table():
    rows = np.arange(ROWS)[:, None]
    angle = 2.0 * np.pi / NFFT * (rows * np.arange(LANES)[None, :])
    return np.concatenate([np.cos(angle), np.sin(angle)], 0).astype(np.float32)


def bin_weights(norm):
    rows = np.arange(HALF)[:, None]
    order = bin_order()[None, :]
    direct = rows + RADIX * order
    mirror = np.where(rows == 0, HALF, RADIX - rows) + RADIX * order
    bins = np.concatenate([direct, mirror], 1)
    return (np.where(bins == 0, 1.0, 2.0) * np.where(bins % 2 == 0, 1.0, -1.0) * norm).astype(np.float32)


def turn(re, im, c, s):
    if abs(c - s) < 1e-12:
        return (re + im) * c, (im - re) * c
    if abs(c + s) < 1e-12:
        return (im - re) * s, -(re + im) * s
    return re * c + im * s, im * c - re * s


def real_fft(x):
    n = len(x)
    if n == 2:
        return [x[0] + x[1], x[0] - x[1]], [None, None]
    er, ei = real_fft(x[0::2])
    odr, odi = real_fft(x[1::2])
    half, quarter = n // 2, n // 4
    re, im = [None] * (half + 1), [None] * (half + 1)
    re[0], re[half] = er[0] + odr[0], er[0] - odr[0]
    re[quarter], im[quarter] = er[quarter], -odr[quarter]
    for k in range(1, quarter):
        angle = 2.0 * math.pi * k / n
        tr, ti = turn(odr[k], odi[k], math.cos(angle), math.sin(angle))
        re[k], im[k] = er[k] + tr, ei[k] + ti
        re[half - k], im[half - k] = er[k] - tr, ti - ei[k]
    return re, im


def real_fft_adjoint(re, im):
    half = len(re) - 1
    n = 2 * half
    if n == 2:
        return [re[0] + re[1], re[0] - re[1]]
    quarter = n // 4
    er, ei = [None] * (quarter + 1), [None] * (quarter + 1)
    odr, odi = [None] * (quarter + 1), [None] * (quarter + 1)
    er[0], odr[0] = re[0] + re[half], re[0] - re[half]
    er[quarter], odr[quarter] = re[quarter], -im[quarter]
    for k in range(1, quarter):
        er[k], ei[k] = re[k] + re[half - k], im[k] - im[half - k]
        tr, ti = re[k] - re[half - k], im[k] + im[half - k]
        angle = 2.0 * math.pi * k / n
        odr[k], odi[k] = turn(tr, ti, math.cos(angle), -math.sin(angle))
    even = real_fft_adjoint(er, ei)
    odd = real_fft_adjoint(odr, odi)
    out = [None] * n
    out[0::2] = even
    out[1::2] = odd
    return out


def matmul(rows, table):
    high = rows.astype(jnp.bfloat16)
    low = (rows - high.astype(jnp.float32)).astype(jnp.bfloat16)
    wide = jnp.concatenate([high, low, high], axis=1)
    return jnp.dot(wide, table, preferred_element_type=jnp.float32)


def lane_ids():
    return lax.broadcasted_iota(jnp.int32, (SUB, LANES), 1)


def lift(x, twist_ref, grid_ref, base):
    re, im = real_fft(x)
    for k in range(ROWS):
        if k == 0:
            zr, zi = re[0], jnp.zeros_like(re[0])
        else:
            c = twist_ref[k : k + 1, :]
            s = twist_ref[ROWS + k : ROWS + k + 1, :]
            if k == HALF:
                zr, zi = re[k] * c, -(re[k] * s)
            else:
                zr, zi = re[k] * c + im[k] * s, im[k] * c - re[k] * s
        spot = pl.ds(base + k * SUB, SUB)
        grid_ref[spot, :LANES] = zr
        grid_ref[spot, LANES:] = zi


def whiten(spec_ref, base):
    first = lane_ids() < QUART
    re, im = [], []
    for k in range(HALF):
        spot = pl.ds(base + k * SUB, SUB)
        r, i = spec_ref[spot, :LANES], spec_ref[spot, LANES:]
        if k == 0:
            last = pl.ds(base + HALF * SUB, SUB)
            r = jnp.where(first, r, spec_ref[last, :LANES])
            i = jnp.where(first, i, spec_ref[last, LANES:])
        re.append(r)
        im.append(i)
    power = re[0] * re[0] + im[0] * im[0]
    for r, i in zip(re[1:], im[1:]):
        power = power + (r * r + i * i)
    power = power + pltpu.roll(power, QUART, 1)
    power = power + pltpu.roll(power, QUART // 2, 1)
    scale = 1.0 / jnp.sqrt(power * (1.0 / BAND) + EPS)
    return [r * scale for r in re], [i * scale for i in im]


def source_stage(windows, me, raw_ref, twist_ref, table_ref, weight_ref, out_ref, grid_ref):
    span = windows * RADIX
    sources = raw_ref.shape[0] // span
    lanes = lane_ids()
    for g in range(sources // SUB):
        match = []
        for w in range(windows):
            own = jnp.broadcast_to(raw_ref[pl.ds(me * span + w * RADIX, 1), :1], (SUB, 1))
            x = [raw_ref[pl.ds(g * SUB * span + w * RADIX + v, SUB, stride=span), :] for v in range(RADIX)]
            match.append(jnp.where(x[0][:, :1] == own, 1.0, 0.0))
            x[0] = jnp.where(lanes == 0, 0.0, x[0])
            lift(x, twist_ref, grid_ref, w * PAD)
        grid_ref[...] = matmul(grid_ref[...], table_ref[...])
        for w in range(windows):
            re, im = whiten(grid_ref, w * PAD)
            for k in range(HALF):
                weight = weight_ref[k : k + 1, :] * match[w]
                spot = pl.ds((w * HALF + k) * sources + g * SUB, SUB)
                out_ref[spot, :LANES] = re[k] * weight
                out_ref[spot, LANES:] = im[k] * weight


def main_kernel(windows, batch, first, blocks, bases, *refs):
    fresh = len(refs) - windows - 4 == 11
    ins, refs = refs[:windows], refs[windows:]
    twist_ref, table_ref, back_ref, weight_ref = refs[:4]
    if fresh:
        raw_hbm, out_ref, kept_ref, source_ref, grid_ref, spec_ref, cross_ref, page_ref, raw_ref, sems, load = refs[4:]
    else:
        kept_ref, _, out_ref, source_ref, grid_ref, spec_ref, cross_ref, page_ref, sems, load = refs[4:]
    sources = source_ref.shape[0] // (windows * HALF)
    if fresh:
        fetch = pltpu.make_async_copy(raw_hbm, raw_ref, load.at[0])
        keep = pltpu.make_async_copy(source_ref, kept_ref, load.at[1])
    else:
        fetch = pltpu.make_async_copy(kept_ref, source_ref, load.at[0])
    fetch.start()
    lower = lane_ids() < QUART
    rounds = SUB // batch
    steps = rounds * (sources // SUB)

    def forward(block):
        for w in range(windows):
            if bases[w] is None:
                x = [ins[w][RADIX + v * SUB : RADIX + (v + 1) * SUB, :] for v in range(RADIX)]
            else:
                spot = pl.ds(pl.multiple_of(bases[w] + block * SUB, SUB), SUB)
                x = [ins[w][spot, v * LANES : (v + 1) * LANES] for v in range(RADIX)]
            lift(x, twist_ref, grid_ref, w * PAD)
        grid_ref[...] = matmul(grid_ref[...], table_ref[...])
        for w in range(windows):
            re, im = whiten(grid_ref, w * PAD)
            for k in range(HALF):
                spec_ref[:, w * HALF + k, :LANES] = re[k]
                spec_ref[:, w * HALF + k, LANES:] = im[k]

    def place(step):
        block, within = lax.div(step, steps), lax.rem(step, steps)
        return block, lax.rem(within, rounds) * batch, pl.multiple_of(lax.div(within, rounds) * SUB, SUB)

    def copy(step, slot, c):
        block, start, group = place(step)
        target = out_ref.at[first + block * SUB + start + c, pl.ds(group, SUB), :]
        return pltpu.make_async_copy(page_ref.at[slot, c], target, sems.at[slot, c])

    def some(step, _):
        slot = lax.rem(step, 2)
        block, start, group = place(step)

        @pl.when(lax.rem(step, steps) == 0)
        def _():
            forward(block)

        if not fresh:
            pl.when(step == 0)(fetch.wait)

        @pl.when(step >= 2)
        def _():
            for c in range(batch):
                copy(step - 2, slot, c).wait()

        def combine(k):
            found = []
            parts = []
            for w in range(windows):
                spot = pl.ds(pl.multiple_of((w * HALF + k) * sources + group, SUB), SUB)
                parts.append((source_ref[spot, :LANES], source_ref[spot, LANES:]))
            for c in range(batch):
                re = im = None
                for w in range(windows):
                    ur, ui = parts[w]
                    row = w * HALF + k
                    sr = spec_ref[start + c, row : row + 1, :LANES]
                    si = spec_ref[start + c, row : row + 1, LANES:]
                    r, i = sr * ur + si * ui, si * ur - sr * ui
                    re, im = (r, i) if re is None else (re + r, im + i)
                found.append((re, im))
            return found

        for c, (re, im) in enumerate(combine(0)):
            cross_ref[pl.ds(c * PAD, SUB), :LANES] = jnp.where(lower, re, 0.0)
            cross_ref[pl.ds(c * PAD, SUB), LANES:] = jnp.where(lower, im, 0.0)
            cross_ref[pl.ds(c * PAD + HALF * SUB, SUB), :LANES] = jnp.where(lower, 0.0, re)
            cross_ref[pl.ds(c * PAD + HALF * SUB, SUB), LANES:] = jnp.where(lower, 0.0, im)
        for k in range(1, HALF):
            for c, (re, im) in enumerate(combine(k)):
                spot = pl.ds(c * PAD + k * SUB, SUB)
                cross_ref[spot, :LANES] = re
                cross_ref[spot, LANES:] = im
        cross_ref[...] = matmul(cross_ref[...], back_ref[...])
        for c in range(batch):
            re, im = [], []
            for k in range(ROWS):
                spot = pl.ds(c * PAD + k * SUB, SUB)
                r, i = cross_ref[spot, :LANES], cross_ref[spot, LANES:]
                if k == 0:
                    i = None
                else:
                    cos = twist_ref[k : k + 1, :]
                    sin = twist_ref[ROWS + k : ROWS + k + 1, :]
                    r, i = r * cos - i * sin, (None if k == HALF else i * cos + r * sin)
                re.append(r)
                im.append(i)
            lags = real_fft_adjoint(re, im)
            for v in range(RADIX):
                page_ref[slot, c, :, v * LANES : (v + 1) * LANES] = lags[v]
            copy(step, slot, c).start()
        return 0

    if fresh:
        fetch.wait()
        source_stage(windows, lax.axis_index("blk"), raw_ref, twist_ref, table_ref, weight_ref, source_ref, grid_ref)
        keep.start()
    every = steps * blocks
    lax.fori_loop(0, every, some, 0)
    for step in range(max(0, every - 2), every):
        for c in range(batch):
            copy(jnp.int32(step), step % 2, c).wait()
    if fresh:
        keep.wait()


def correlations(pieces, tables, total, first, rows, raw=None, source=None, before=None, batch=4):
    windows = len(pieces)
    sources = raw.shape[0] // (windows * RADIX) if source is None else source.shape[0] // (windows * HALF)
    args = [array for array, _ in pieces] + list(tables)
    inside, outside = pl.BlockSpec(memory_space=pltpu.VMEM), pl.BlockSpec(memory_space=pltpu.HBM)
    specs = [inside] * len(args)
    shapes = [jax.ShapeDtypeStruct((total, sources, NFFT), jnp.float32)]
    spectra = (windows * HALF * sources, 2 * LANES)
    scratch = [
        pltpu.VMEM(spectra, jnp.float32),
        pltpu.VMEM((windows * PAD, 2 * LANES), jnp.float32),
        pltpu.VMEM((SUB, windows * HALF, 2 * LANES), jnp.float32),
        pltpu.VMEM((batch * PAD, 2 * LANES), jnp.float32),
        pltpu.VMEM((2, batch, SUB, NFFT), jnp.float32),
        pltpu.SemaphoreType.DMA((2, batch)),
        pltpu.SemaphoreType.DMA((2,)),
    ]
    aliases = {}
    if source is None:
        args.append(raw)
        specs.append(outside)
        shapes.append(jax.ShapeDtypeStruct(spectra, jnp.float32))
        scratch.insert(5, pltpu.VMEM(raw.shape, jnp.float32))
    else:
        aliases = {len(args) + 1: 0}
        args += [source, before]
        specs += [outside, pl.BlockSpec(memory_space=pl.ANY)]
    return pl.pallas_call(
        functools.partial(main_kernel, windows, batch, first, rows // SUB, [base for _, base in pieces]),
        out_shape=shapes,
        in_specs=specs,
        out_specs=[outside] * len(shapes),
        scratch_shapes=scratch,
        input_output_aliases=aliases,
        compiler_params=pltpu.CompilerParams(vmem_limit_bytes=32 * 2**20),
        name=f"lags_{first}",
    )(*args)


def all_tables(norm):
    forward, back = dft_tables()
    return tuple(jnp.asarray(table) for table in (twist_table(), forward, back, bin_weights(norm)))


def live_window(gaps_ref):
    live, most = jnp.int32(0), gaps_ref[1, 0, 0]
    for slot in range(1, gaps_ref.shape[2]):
        better = gaps_ref[1, 0, slot] > most
        live = jnp.where(better, slot, live)
        most = jnp.where(better, gaps_ref[1, 0, slot], most)
    return live, gaps_ref[0, 0, live], most


def taper_kernel(mine, windows, lead, rest, gaps_hbm, taper_hbm, records_ref, *refs):
    outs, (gaps_ref, taper_ref, head_ref, load, sems) = refs[:-5], refs[-5:]
    here = lax.axis_index("tm")
    known = pltpu.make_async_copy(gaps_hbm, gaps_ref, load.at[0])
    shape = pltpu.make_async_copy(taper_hbm, taper_ref, load.at[1])
    known.start()
    shape.start()
    heads = [lax.rem(here + step, windows) * mine for step in lead] + [jnp.int32(0)] * bool(lead)
    copies = []
    for slot in range(gaps_ref.shape[2] if lead else 0):
        for n, base in enumerate(heads):
            spot = pl.ds(pl.multiple_of(base, SUB), SUB)
            source = records_ref.at[spot, pl.ds(slot * NFFT, NFFT)]
            copies.append(pltpu.make_async_copy(source, head_ref.at[slot, n], sems.at[len(copies)]))
    for copy in copies:
        copy.start()
    known.wait()
    live, start, most = live_window(gaps_ref)
    column = pl.ds(pl.multiple_of(live * NFFT, NFFT), NFFT)
    for n, (step, first, rows) in enumerate(rest):
        base = pl.multiple_of(lax.rem(here + step, windows) * mine + first, SUB)
        copies.append(pltpu.make_async_copy(records_ref.at[pl.ds(base, rows), column], outs[n], sems.at[n]))
        copies[-1].start()
    shape.wait()
    spots = lax.broadcasted_iota(jnp.int32, (1, NFFT), 1)
    taper = jnp.where((spots >= start) & (spots < start + most), taper_ref[...], 0.0)
    if lead:
        for copy in copies:
            copy.wait()
        line = jnp.where(spots == 0, live.astype(jnp.float32), head_ref[live, len(lead), :1, :] * taper)
        for v in range(RADIX):
            lanes = slice(v * LANES, (v + 1) * LANES)
            for n in range(len(lead)):
                outs[n][v : v + 1, :] = line[:, lanes]
                outs[n][RADIX + v * SUB : RADIX + (v + 1) * SUB, :] = head_ref[live, n, :, lanes] * taper[:, lanes]
            outs[len(lead)][v : v + 1, :] = line[:, lanes]
        return
    for n, copy in enumerate(copies):
        copy.wait()
        for r in range(0, outs[n].shape[0], SUB):
            outs[n][r : r + SUB, :] = outs[n][r : r + SUB, :] * taper


def tapered(records, gaps, mine, windows, lead, rest):
    spots = np.arange(NFFT)
    slots = gaps.shape[2]
    taper = jnp.asarray((0.5 - 0.5 * np.cos(2.0 * np.pi / NFFT * spots)).astype(np.float32)[None])
    shapes = [(RADIX * (1 + SUB), LANES)] * len(lead) + [(RADIX, LANES)] * bool(lead) + [(rows, NFFT) for _, _, rows in rest]
    args = [pltpu.with_memory_space_constraint(array, pltpu.HBM) for array in (gaps, taper, records)]
    return pl.pallas_call(
        functools.partial(taper_kernel, mine, windows, lead, rest),
        out_shape=[jax.ShapeDtypeStruct(shape, jnp.float32) for shape in shapes],
        in_specs=[pl.BlockSpec(memory_space=pltpu.HBM)] * 3,
        out_specs=[pl.BlockSpec(memory_space=pltpu.VMEM) for _ in shapes],
        scratch_shapes=[
            pltpu.SMEM(gaps.shape, jnp.int32),
            pltpu.VMEM(taper.shape, jnp.float32),
            pltpu.VMEM((slots, 1 + len(lead), SUB, NFFT), jnp.float32),
            pltpu.SemaphoreType.DMA((2,)),
            pltpu.SemaphoreType.DMA((max(len(rest), slots * (1 + len(lead))),)),
        ],
        compiler_params=pltpu.CompilerParams(vmem_limit_bytes=16 * 2**20),
        name="taper_lead" if lead else "taper",
    )(*args)


def shards(records, gaps):
    width = records.shape[0]
    slots = records.shape[1] // NFFT
    windows = lax.axis_size("tm")
    mine = width // windows
    cut = mine - SUB

    def shift(array, step):
        pairs = [(i, (i + step) % windows) for i in range(windows)]
        return lax.ppermute(array, "tm", pairs)

    steps = list(range(1, windows))
    order = sorted(steps, key=lambda d: -min(d, windows - d))
    *lead, row = tapered(records, gaps, mine, windows, steps, [])
    lead = dict(zip(steps, lead))
    lead = {d: shift(lead[d], d) for d in order}
    rows = jnp.stack([row] + [lead[d][:RADIX] for d in steps])

    single, split = order[-1], order[:-1]
    rest = [(d, SUB, cut - SUB) for d in split] + [(single, SUB, mine - SUB)] + [(d, cut, SUB) for d in split] + [(0, 0, mine)]
    *bulk, own = tapered(records, gaps, mine, windows, [], rest)
    early, late = bulk[: len(steps)], bulk[len(steps) :]
    rows, late = lax.optimization_barrier((rows, late))
    raw = lax.all_gather(rows, "blk", axis=0, tiled=False)
    raw = raw.reshape(-1, LANES)
    early = {d: shift(array, d) for d, array in zip(order, early)}
    late = {d: shift(array, d) for d, array in zip(split, late)}

    tables = all_tables(1.0 / math.sqrt(NFFT * slots * windows))
    pieces = [(own, 0)] + [(lead[d], None) for d in steps]
    more = [(own, SUB)] + [(early[d], 0) for d in steps]
    out, source = correlations(pieces, tables, mine, 0, SUB, raw=raw)
    (out,) = correlations(more, tables, mine, SUB, cut - SUB, source=source, before=out)
    pieces = [(own, cut)] + [(late[d], 0) if d in late else (early[d], cut - SUB) for d in steps]
    return correlations(pieces, tables, mine, cut, SUB, source=source, before=out)[0]


def solution(mesh):
    in_specs = (P("blk", "tm"), P(None, "blk", "tm"))
    out_specs = P(("blk", "tm"), None, None)
    return jax.shard_map(shards, mesh=mesh, in_specs=in_specs, out_specs=out_specs, check_vma=False)
```

```python
import functools
import math

import jax
import jax.numpy as jnp
import numpy as np
from jax import lax
from jax.experimental import pallas as pl
from jax.experimental.pallas import tpu as pltpu
from jax.sharding import PartitionSpec as P

NFFT = 4096
BAND = 64
EPS = 1e-05
LANES = 128
SUB = 8
RADIX = NFFT // LANES
HALF = RADIX // 2
ROWS = HALF + 1
QUART = LANES // 2
PAD = ROWS * SUB


def split_bf16(table):
    high = table.astype(jnp.bfloat16)
    low = (table - high.astype(np.float32)).astype(jnp.bfloat16)
    return high, low


def bin_order():
    half = np.arange(QUART // 2)
    return np.concatenate([2 * half, 2 * half + 1])


def dft_tables():
    spots = np.arange(LANES)[:, None]
    order = bin_order()[None, :]
    direct = 2.0 * np.pi / LANES * (spots * order % LANES)
    mirror = 2.0 * np.pi / LANES * (spots * (LANES - 1 - order) % LANES)
    upper = np.concatenate([np.cos(direct), np.cos(mirror), -np.sin(direct), np.sin(mirror)], 1)
    lower = np.concatenate([np.sin(direct), np.sin(mirror), np.cos(direct), -np.cos(mirror)], 1)
    full = np.concatenate([upper, lower], 0).astype(np.float32)
    tables = []
    for one in (full, full.T):
        high, low = split_bf16(one)
        tables.append(np.concatenate([high, high, low], 0))
    return tables


def twist_table():
    rows = np.arange(ROWS)[:, None]
    angle = 2.0 * np.pi / NFFT * (rows * np.arange(LANES)[None, :])
    return np.concatenate([np.cos(angle), np.sin(angle)], 0).astype(np.float32)


def bin_weights(norm):
    rows = np.arange(HALF)[:, None]
    order = bin_order()[None, :]
    direct = rows + RADIX * order
    mirror = np.where(rows == 0, HALF, RADIX - rows) + RADIX * order
    bins = np.concatenate([direct, mirror], 1)
    return (np.where(bins == 0, 1.0, 2.0) * np.where(bins % 2 == 0, 1.0, -1.0) * norm).astype(np.float32)


def turn(re, im, c, s):
    if abs(c - s) < 1e-12:
        return (re + im) * c, (im - re) * c
    if abs(c + s) < 1e-12:
        return (im - re) * s, -(re + im) * s
    return re * c + im * s, im * c - re * s


def real_fft(x):
    n = len(x)
    if n == 2:
        return [x[0] + x[1], x[0] - x[1]], [None, None]
    er, ei = real_fft(x[0::2])
    odr, odi = real_fft(x[1::2])
    half, quarter = n // 2, n // 4
    re, im = [None] * (half + 1), [None] * (half + 1)
    re[0], re[half] = er[0] + odr[0], er[0] - odr[0]
    re[quarter], im[quarter] = er[quarter], -odr[quarter]
    for k in range(1, quarter):
        angle = 2.0 * math.pi * k / n
        tr, ti = turn(odr[k], odi[k], math.cos(angle), math.sin(angle))
        re[k], im[k] = er[k] + tr, ei[k] + ti
        re[half - k], im[half - k] = er[k] - tr, ti - ei[k]
    return re, im


def real_fft_adjoint(re, im):
    half = len(re) - 1
    n = 2 * half
    if n == 2:
        return [re[0] + re[1], re[0] - re[1]]
    quarter = n // 4
    er, ei = [None] * (quarter + 1), [None] * (quarter + 1)
    odr, odi = [None] * (quarter + 1), [None] * (quarter + 1)
    er[0], odr[0] = re[0] + re[half], re[0] - re[half]
    er[quarter], odr[quarter] = re[quarter], -im[quarter]
    for k in range(1, quarter):
        er[k], ei[k] = re[k] + re[half - k], im[k] - im[half - k]
        tr, ti = re[k] - re[half - k], im[k] + im[half - k]
        angle = 2.0 * math.pi * k / n
        odr[k], odi[k] = turn(tr, ti, math.cos(angle), -math.sin(angle))
    even = real_fft_adjoint(er, ei)
    odd = real_fft_adjoint(odr, odi)
    out = [None] * n
    out[0::2] = even
    out[1::2] = odd
    return out


def matmul(rows, table):
    high = rows.astype(jnp.bfloat16)
    low = (rows - high.astype(jnp.float32)).astype(jnp.bfloat16)
    wide = jnp.concatenate([high, low, high], axis=1)
    return jnp.dot(wide, table, preferred_element_type=jnp.float32)


def lane_ids():
    return lax.broadcasted_iota(jnp.int32, (SUB, LANES), 1)


def lift(x, twist_ref, grid_ref, base):
    re, im = real_fft(x)
    for k in range(ROWS):
        if k == 0:
            zr, zi = re[0], jnp.zeros_like(re[0])
        else:
            c = twist_ref[k : k + 1, :]
            s = twist_ref[ROWS + k : ROWS + k + 1, :]
            if k == HALF:
                zr, zi = re[k] * c, -(re[k] * s)
            else:
                zr, zi = re[k] * c + im[k] * s, im[k] * c - re[k] * s
        spot = pl.ds(base + k * SUB, SUB)
        grid_ref[spot, :LANES] = zr
        grid_ref[spot, LANES:] = zi


def whiten(spec_ref, base):
    first = lane_ids() < QUART
    re, im = [], []
    for k in range(HALF):
        spot = pl.ds(base + k * SUB, SUB)
        r, i = spec_ref[spot, :LANES], spec_ref[spot, LANES:]
        if k == 0:
            last = pl.ds(base + HALF * SUB, SUB)
            r = jnp.where(first, r, spec_ref[last, :LANES])
            i = jnp.where(first, i, spec_ref[last, LANES:])
        re.append(r)
        im.append(i)
    power = re[0] * re[0] + im[0] * im[0]
    for r, i in zip(re[1:], im[1:]):
        power = power + (r * r + i * i)
    power = power + pltpu.roll(power, QUART, 1)
    power = power + pltpu.roll(power, QUART // 2, 1)
    scale = 1.0 / jnp.sqrt(power * (1.0 / BAND) + EPS)
    return [r * scale for r in re], [i * scale for i in im]


def source_stage(windows, me, raw_ref, twist_ref, table_ref, weight_ref, out_ref, grid_ref):
    span = windows * RADIX
    sources = raw_ref.shape[0] // span
    lanes = lane_ids()
    for g in range(sources // SUB):
        match = []
        for w in range(windows):
            own = jnp.broadcast_to(raw_ref[pl.ds(me * span + w * RADIX, 1), :1], (SUB, 1))
            x = [raw_ref[pl.ds(g * SUB * span + w * RADIX + v, SUB, stride=span), :] for v in range(RADIX)]
            match.append(jnp.where(x[0][:, :1] == own, 1.0, 0.0))
            x[0] = jnp.where(lanes == 0, 0.0, x[0])
            lift(x, twist_ref, grid_ref, w * PAD)
        grid_ref[...] = matmul(grid_ref[...], table_ref[...])
        for w in range(windows):
            re, im = whiten(grid_ref, w * PAD)
            for k in range(HALF):
                weight = weight_ref[k : k + 1, :] * match[w]
                spot = pl.ds((w * HALF + k) * sources + g * SUB, SUB)
                out_ref[spot, :LANES] = re[k] * weight
                out_ref[spot, LANES:] = im[k] * weight


def main_kernel(windows, batch, first, blocks, bases, *refs):
    fresh = len(refs) - windows - 4 == 11
    ins, refs = refs[:windows], refs[windows:]
    twist_ref, table_ref, back_ref, weight_ref = refs[:4]
    if fresh:
        raw_hbm, out_ref, kept_ref, source_ref, grid_ref, spec_ref, cross_ref, page_ref, raw_ref, sems, load = refs[4:]
    else:
        kept_ref, _, out_ref, source_ref, grid_ref, spec_ref, cross_ref, page_ref, sems, load = refs[4:]
    sources = source_ref.shape[0] // (windows * HALF)
    if fresh:
        fetch = pltpu.make_async_copy(raw_hbm, raw_ref, load.at[0])
        keep = pltpu.make_async_copy(source_ref, kept_ref, load.at[1])
    else:
        fetch = pltpu.make_async_copy(kept_ref, source_ref, load.at[0])
    fetch.start()
    lower = lane_ids() < QUART
    rounds = SUB // batch
    steps = rounds * (sources // SUB)

    def forward(block):
        for w in range(windows):
            if bases[w] is None:
                x = [ins[w][RADIX + v * SUB : RADIX + (v + 1) * SUB, :] for v in range(RADIX)]
            else:
                spot = pl.ds(pl.multiple_of(bases[w] + block * SUB, SUB), SUB)
                x = [ins[w][spot, v * LANES : (v + 1) * LANES] for v in range(RADIX)]
            lift(x, twist_ref, grid_ref, w * PAD)
        grid_ref[...] = matmul(grid_ref[...], table_ref[...])
        for w in range(windows):
            re, im = whiten(grid_ref, w * PAD)
            for k in range(HALF):
                spec_ref[:, w * HALF + k, :LANES] = re[k]
                spec_ref[:, w * HALF + k, LANES:] = im[k]

    def place(step):
        block, within = lax.div(step, steps), lax.rem(step, steps)
        return block, lax.rem(within, rounds) * batch, pl.multiple_of(lax.div(within, rounds) * SUB, SUB)

    def copy(step, slot, c):
        block, start, group = place(step)
        target = out_ref.at[first + block * SUB + start + c, pl.ds(group, SUB), :]
        return pltpu.make_async_copy(page_ref.at[slot, c], target, sems.at[slot, c])

    def some(step, _):
        slot = lax.rem(step, 2)
        block, start, group = place(step)

        @pl.when(lax.rem(step, steps) == 0)
        def _():
            forward(block)

        if not fresh:
            pl.when(step == 0)(fetch.wait)

        @pl.when(step >= 2)
        def _():
            for c in range(batch):
                copy(step - 2, slot, c).wait()

        def combine(k):
            found = []
            parts = []
            for w in range(windows):
                spot = pl.ds(pl.multiple_of((w * HALF + k) * sources + group, SUB), SUB)
                parts.append((source_ref[spot, :LANES], source_ref[spot, LANES:]))
            for c in range(batch):
                re = im = None
                for w in range(windows):
                    ur, ui = parts[w]
                    row = w * HALF + k
                    sr = spec_ref[start + c, row : row + 1, :LANES]
                    si = spec_ref[start + c, row : row + 1, LANES:]
                    r, i = sr * ur + si * ui, si * ur - sr * ui
                    re, im = (r, i) if re is None else (re + r, im + i)
                found.append((re, im))
            return found

        for c, (re, im) in enumerate(combine(0)):
            cross_ref[pl.ds(c * PAD, SUB), :LANES] = jnp.where(lower, re, 0.0)
            cross_ref[pl.ds(c * PAD, SUB), LANES:] = jnp.where(lower, im, 0.0)
            cross_ref[pl.ds(c * PAD + HALF * SUB, SUB), :LANES] = jnp.where(lower, 0.0, re)
            cross_ref[pl.ds(c * PAD + HALF * SUB, SUB), LANES:] = jnp.where(lower, 0.0, im)
        for k in range(1, HALF):
            for c, (re, im) in enumerate(combine(k)):
                spot = pl.ds(c * PAD + k * SUB, SUB)
                cross_ref[spot, :LANES] = re
                cross_ref[spot, LANES:] = im
        cross_ref[...] = matmul(cross_ref[...], back_ref[...])
        for c in range(batch):
            re, im = [], []
            for k in range(ROWS):
                spot = pl.ds(c * PAD + k * SUB, SUB)
                r, i = cross_ref[spot, :LANES], cross_ref[spot, LANES:]
                if k == 0:
                    i = None
                else:
                    cos = twist_ref[k : k + 1, :]
                    sin = twist_ref[ROWS + k : ROWS + k + 1, :]
                    r, i = r * cos - i * sin, (None if k == HALF else i * cos + r * sin)
                re.append(r)
                im.append(i)
            lags = real_fft_adjoint(re, im)
            for v in range(RADIX):
                page_ref[slot, c, :, v * LANES : (v + 1) * LANES] = lags[v]
            copy(step, slot, c).start()
        return 0

    if fresh:
        fetch.wait()
        source_stage(windows, lax.axis_index("blk"), raw_ref, twist_ref, table_ref, weight_ref, source_ref, grid_ref)
        keep.start()
    every = steps * blocks
    lax.fori_loop(0, every, some, 0)
    for step in range(max(0, every - 2), every):
        for c in range(batch):
            copy(jnp.int32(step), step % 2, c).wait()
    if fresh:
        keep.wait()


def correlations(pieces, tables, total, first, rows, raw=None, source=None, before=None, batch=4):
    windows = len(pieces)
    sources = raw.shape[0] // (windows * RADIX) if source is None else source.shape[0] // (windows * HALF)
    args = [array for array, _ in pieces] + list(tables)
    inside, outside = pl.BlockSpec(memory_space=pltpu.VMEM), pl.BlockSpec(memory_space=pltpu.HBM)
    specs = [inside] * len(args)
    shapes = [jax.ShapeDtypeStruct((total, sources, NFFT), jnp.float32)]
    spectra = (windows * HALF * sources, 2 * LANES)
    scratch = [
        pltpu.VMEM(spectra, jnp.float32),
        pltpu.VMEM((windows * PAD, 2 * LANES), jnp.float32),
        pltpu.VMEM((SUB, windows * HALF, 2 * LANES), jnp.float32),
        pltpu.VMEM((batch * PAD, 2 * LANES), jnp.float32),
        pltpu.VMEM((2, batch, SUB, NFFT), jnp.float32),
        pltpu.SemaphoreType.DMA((2, batch)),
        pltpu.SemaphoreType.DMA((2,)),
    ]
    aliases = {}
    if source is None:
        args.append(raw)
        specs.append(outside)
        shapes.append(jax.ShapeDtypeStruct(spectra, jnp.float32))
        scratch.insert(5, pltpu.VMEM(raw.shape, jnp.float32))
    else:
        aliases = {len(args) + 1: 0}
        args += [source, before]
        specs += [outside, pl.BlockSpec(memory_space=pl.ANY)]
    return pl.pallas_call(
        functools.partial(main_kernel, windows, batch, first, rows // SUB, [base for _, base in pieces]),
        out_shape=shapes,
        in_specs=specs,
        out_specs=[outside] * len(shapes),
        scratch_shapes=scratch,
        input_output_aliases=aliases,
        compiler_params=pltpu.CompilerParams(vmem_limit_bytes=32 * 2**20),
        name=f"lags_{first}",
    )(*args)


def all_tables(norm):
    forward, back = dft_tables()
    return tuple(jnp.asarray(table) for table in (twist_table(), forward, back, bin_weights(norm)))


def live_window(gaps_ref):
    live, most = jnp.int32(0), gaps_ref[1, 0, 0]
    for slot in range(1, gaps_ref.shape[2]):
        better = gaps_ref[1, 0, slot] > most
        live = jnp.where(better, slot, live)
        most = jnp.where(better, gaps_ref[1, 0, slot], most)
    return live, gaps_ref[0, 0, live], most


def taper_kernel(mine, windows, lead, rest, gaps_hbm, taper_hbm, records_ref, *refs):
    outs, (gaps_ref, taper_ref, head_ref, load, sems) = refs[:-5], refs[-5:]
    here = lax.axis_index("tm")
    known = pltpu.make_async_copy(gaps_hbm, gaps_ref, load.at[0])
    shape = pltpu.make_async_copy(taper_hbm, taper_ref, load.at[1])
    known.start()
    shape.start()
    heads = [lax.rem(here + step, windows) * mine for step in lead] + [jnp.int32(0)] * bool(lead)
    copies = []
    for slot in range(gaps_ref.shape[2] if lead else 0):
        for n, base in enumerate(heads):
            spot = pl.ds(pl.multiple_of(base, SUB), SUB)
            source = records_ref.at[spot, pl.ds(slot * NFFT, NFFT)]
            copies.append(pltpu.make_async_copy(source, head_ref.at[slot, n], sems.at[len(copies)]))
    for copy in copies:
        copy.start()
    known.wait()
    live, start, most = live_window(gaps_ref)
    column = pl.ds(pl.multiple_of(live * NFFT, NFFT), NFFT)
    for n, (step, first, rows) in enumerate(rest):
        base = pl.multiple_of(lax.rem(here + step, windows) * mine + first, SUB)
        copies.append(pltpu.make_async_copy(records_ref.at[pl.ds(base, rows), column], outs[n], sems.at[n]))
        copies[-1].start()
    shape.wait()
    spots = lax.broadcasted_iota(jnp.int32, (1, NFFT), 1)
    taper = jnp.where((spots >= start) & (spots < start + most), taper_ref[...], 0.0)
    if lead:
        for copy in copies:
            copy.wait()
        line = jnp.where(spots == 0, live.astype(jnp.float32), head_ref[live, len(lead), :1, :] * taper)
        for v in range(RADIX):
            lanes = slice(v * LANES, (v + 1) * LANES)
            for n in range(len(lead)):
                outs[n][v : v + 1, :] = line[:, lanes]
                outs[n][RADIX + v * SUB : RADIX + (v + 1) * SUB, :] = head_ref[live, n, :, lanes] * taper[:, lanes]
            outs[len(lead)][v : v + 1, :] = line[:, lanes]
        return
    for n, copy in enumerate(copies):
        copy.wait()
        for r in range(0, outs[n].shape[0], SUB):
            outs[n][r : r + SUB, :] = outs[n][r : r + SUB, :] * taper


def tapered(records, gaps, mine, windows, lead, rest):
    spots = np.arange(NFFT)
    slots = gaps.shape[2]
    taper = jnp.asarray((0.5 - 0.5 * np.cos(2.0 * np.pi / NFFT * spots)).astype(np.float32)[None])
    shapes = [(RADIX * (1 + SUB), LANES)] * len(lead) + [(RADIX, LANES)] * bool(lead) + [(rows, NFFT) for _, _, rows in rest]
    args = [pltpu.with_memory_space_constraint(array, pltpu.HBM) for array in (gaps, taper, records)]
    return pl.pallas_call(
        functools.partial(taper_kernel, mine, windows, lead, rest),
        out_shape=[jax.ShapeDtypeStruct(shape, jnp.float32) for shape in shapes],
        in_specs=[pl.BlockSpec(memory_space=pltpu.HBM)] * 3,
        out_specs=[pl.BlockSpec(memory_space=pltpu.VMEM) for _ in shapes],
        scratch_shapes=[
            pltpu.SMEM(gaps.shape, jnp.int32),
            pltpu.VMEM(taper.shape, jnp.float32),
            pltpu.VMEM((slots, 1 + len(lead), SUB, NFFT), jnp.float32),
            pltpu.SemaphoreType.DMA((2,)),
            pltpu.SemaphoreType.DMA((max(len(rest), slots * (1 + len(lead))),)),
        ],
        compiler_params=pltpu.CompilerParams(vmem_limit_bytes=16 * 2**20),
        name="taper_lead" if lead else "taper",
    )(*args)


def shards(records, gaps):
    width = records.shape[0]
    slots = records.shape[1] // NFFT
    windows = lax.axis_size("tm")
    mine = width // windows
    cut = mine - SUB

    def shift(array, step):
        pairs = [(i, (i + step) % windows) for i in range(windows)]
        return lax.ppermute(array, "tm", pairs)

    steps = list(range(1, windows))
    order = sorted(steps, key=lambda d: (-min(d, windows - d), -d))
    *lead, row = tapered(records, gaps, mine, windows, steps, [])
    lead = dict(zip(steps, lead))
    lead = {d: shift(lead[d], d) for d in [order[0], order[1], order[2]]}
    rows = jnp.stack([row] + [lead[d][:RADIX] for d in steps])

    split = order
    first = [order[0], order[1], order[2]]
    rest = [(d, SUB, (cut if d in split else mine) - SUB) for d in first] + [(d, cut, SUB) for d in split] + [(0, 0, mine)]
    *bulk, own = tapered(records, gaps, mine, windows, [], rest)
    early, late = bulk[: len(steps)], bulk[len(steps) :]
    raw = lax.all_gather(rows, "blk", axis=0, tiled=False)
    raw, late = lax.optimization_barrier((raw, late))
    raw = raw.reshape(-1, LANES)
    early = {d: shift(array, d) for d, array in zip(first, early)}
    late = {d: shift(array, d) for d, array in zip(split, late)}

    tables = all_tables(1.0 / math.sqrt(NFFT * slots * windows))
    pieces = [(own, 0)] + [(lead[d], None) for d in steps]
    more = [(own, SUB)] + [(early[d], 0) for d in steps]
    out, source = correlations(pieces, tables, mine, 0, SUB, raw=raw)
    (out,) = correlations(more, tables, mine, SUB, cut - SUB, source=source, before=out)
    pieces = [(own, cut)] + [(late[d], 0) if d in late else (early[d], cut - SUB) for d in steps]
    return correlations(pieces, tables, mine, cut, SUB, source=source, before=out)[0]


def solution(mesh):
    in_specs = (P("blk", "tm"), P(None, "blk", "tm"))
    out_specs = P(("blk", "tm"), None, None)
    return jax.shard_map(shards, mesh=mesh, in_specs=in_specs, out_specs=out_specs, check_vma=False)
```

```python
import functools
import math

import jax
import jax.numpy as jnp
import numpy as np
from jax import lax
from jax.experimental import pallas as pl
from jax.experimental.pallas import tpu as pltpu
from jax.sharding import PartitionSpec as P

NFFT = 4096
BAND = 64
EPS = 1e-05
LANES = 128
SUB = 8
RADIX = NFFT // LANES
HALF = RADIX // 2
ROWS = HALF + 1
QUART = LANES // 2
PAD = ROWS * SUB


def split_bf16(table):
    high = table.astype(jnp.bfloat16)
    low = (table - high.astype(np.float32)).astype(jnp.bfloat16)
    return high, low


def bin_order():
    half = np.arange(QUART // 2)
    return np.concatenate([2 * half, 2 * half + 1])


def dft_tables():
    spots = np.arange(LANES)[:, None]
    order = bin_order()[None, :]
    direct = 2.0 * np.pi / LANES * (spots * order % LANES)
    mirror = 2.0 * np.pi / LANES * (spots * (LANES - 1 - order) % LANES)
    upper = np.concatenate([np.cos(direct), np.cos(mirror), -np.sin(direct), np.sin(mirror)], 1)
    lower = np.concatenate([np.sin(direct), np.sin(mirror), np.cos(direct), -np.cos(mirror)], 1)
    full = np.concatenate([upper, lower], 0).astype(np.float32)
    tables = []
    for one in (full, full.T):
        high, low = split_bf16(one)
        tables.append(np.concatenate([high, high, low], 0))
    return tables


def twist_table():
    rows = np.arange(ROWS)[:, None]
    angle = 2.0 * np.pi / NFFT * (rows * np.arange(LANES)[None, :])
    return np.concatenate([np.cos(angle), np.sin(angle)], 0).astype(np.float32)


def bin_weights(norm):
    rows = np.arange(HALF)[:, None]
    order = bin_order()[None, :]
    direct = rows + RADIX * order
    mirror = np.where(rows == 0, HALF, RADIX - rows) + RADIX * order
    bins = np.concatenate([direct, mirror], 1)
    return (np.where(bins == 0, 1.0, 2.0) * np.where(bins % 2 == 0, 1.0, -1.0) * norm).astype(np.float32)


def turn(re, im, c, s):
    if abs(c - s) < 1e-12:
        return (re + im) * c, (im - re) * c
    if abs(c + s) < 1e-12:
        return (im - re) * s, -(re + im) * s
    return re * c + im * s, im * c - re * s


def real_fft(x):
    n = len(x)
    if n == 2:
        return [x[0] + x[1], x[0] - x[1]], [None, None]
    er, ei = real_fft(x[0::2])
    odr, odi = real_fft(x[1::2])
    half, quarter = n // 2, n // 4
    re, im = [None] * (half + 1), [None] * (half + 1)
    re[0], re[half] = er[0] + odr[0], er[0] - odr[0]
    re[quarter], im[quarter] = er[quarter], -odr[quarter]
    for k in range(1, quarter):
        angle = 2.0 * math.pi * k / n
        tr, ti = turn(odr[k], odi[k], math.cos(angle), math.sin(angle))
        re[k], im[k] = er[k] + tr, ei[k] + ti
        re[half - k], im[half - k] = er[k] - tr, ti - ei[k]
    return re, im


def real_fft_adjoint(re, im):
    half = len(re) - 1
    n = 2 * half
    if n == 2:
        return [re[0] + re[1], re[0] - re[1]]
    quarter = n // 4
    er, ei = [None] * (quarter + 1), [None] * (quarter + 1)
    odr, odi = [None] * (quarter + 1), [None] * (quarter + 1)
    er[0], odr[0] = re[0] + re[half], re[0] - re[half]
    er[quarter], odr[quarter] = re[quarter], -im[quarter]
    for k in range(1, quarter):
        er[k], ei[k] = re[k] + re[half - k], im[k] - im[half - k]
        tr, ti = re[k] - re[half - k], im[k] + im[half - k]
        angle = 2.0 * math.pi * k / n
        odr[k], odi[k] = turn(tr, ti, math.cos(angle), -math.sin(angle))
    even = real_fft_adjoint(er, ei)
    odd = real_fft_adjoint(odr, odi)
    out = [None] * n
    out[0::2] = even
    out[1::2] = odd
    return out


def matmul(rows, table):
    high = rows.astype(jnp.bfloat16)
    low = (rows - high.astype(jnp.float32)).astype(jnp.bfloat16)
    wide = jnp.concatenate([high, low, high], axis=1)
    return jnp.dot(wide, table, preferred_element_type=jnp.float32)


def lane_ids():
    return lax.broadcasted_iota(jnp.int32, (SUB, LANES), 1)


def lift(x, twist_ref, grid_ref, base):
    re, im = real_fft(x)
    for k in range(ROWS):
        if k == 0:
            zr, zi = re[0], jnp.zeros_like(re[0])
        else:
            c = twist_ref[k : k + 1, :]
            s = twist_ref[ROWS + k : ROWS + k + 1, :]
            if k == HALF:
                zr, zi = re[k] * c, -(re[k] * s)
            else:
                zr, zi = re[k] * c + im[k] * s, im[k] * c - re[k] * s
        spot = pl.ds(base + k * SUB, SUB)
        grid_ref[spot, :LANES] = zr
        grid_ref[spot, LANES:] = zi


def whiten(spec_ref, base):
    first = lane_ids() < QUART
    re, im = [], []
    for k in range(HALF):
        spot = pl.ds(base + k * SUB, SUB)
        r, i = spec_ref[spot, :LANES], spec_ref[spot, LANES:]
        if k == 0:
            last = pl.ds(base + HALF * SUB, SUB)
            r = jnp.where(first, r, spec_ref[last, :LANES])
            i = jnp.where(first, i, spec_ref[last, LANES:])
        re.append(r)
        im.append(i)
    power = re[0] * re[0] + im[0] * im[0]
    for r, i in zip(re[1:], im[1:]):
        power = power + (r * r + i * i)
    power = power + pltpu.roll(power, QUART, 1)
    power = power + pltpu.roll(power, QUART // 2, 1)
    scale = lax.rsqrt(power * (1.0 / BAND) + EPS)
    return [r * scale for r in re], [i * scale for i in im]


def source_stage(windows, me, raw_ref, twist_ref, table_ref, weight_ref, out_ref, grid_ref):
    span = windows * RADIX
    sources = raw_ref.shape[0] // span
    lanes = lane_ids()
    for g in range(sources // SUB):
        match = []
        for w in range(windows):
            own = jnp.broadcast_to(raw_ref[pl.ds(me * span + w * RADIX, 1), :1], (SUB, 1))
            x = [raw_ref[pl.ds(g * SUB * span + w * RADIX + v, SUB, stride=span), :] for v in range(RADIX)]
            match.append(jnp.where(x[0][:, :1] == own, 1.0, 0.0))
            x[0] = jnp.where(lanes == 0, 0.0, x[0])
            lift(x, twist_ref, grid_ref, w * PAD)
        grid_ref[...] = matmul(grid_ref[...], table_ref[...])
        for w in range(windows):
            re, im = whiten(grid_ref, w * PAD)
            for k in range(HALF):
                weight = weight_ref[k : k + 1, :] * match[w]
                spot = pl.ds((w * HALF + k) * sources + g * SUB, SUB)
                out_ref[spot, :LANES] = re[k] * weight
                out_ref[spot, LANES:] = im[k] * weight


def main_kernel(windows, batch, first, blocks, bases, *refs):
    fresh = len(refs) - windows - 4 == 11
    ins, refs = refs[:windows], refs[windows:]
    twist_ref, table_ref, back_ref, weight_ref = refs[:4]
    if fresh:
        raw_hbm, out_ref, kept_ref, source_ref, grid_ref, spec_ref, cross_ref, page_ref, raw_ref, sems, load = refs[4:]
    else:
        kept_ref, _, out_ref, source_ref, grid_ref, spec_ref, cross_ref, page_ref, sems, load = refs[4:]
    sources = source_ref.shape[0] // (windows * HALF)
    if fresh:
        fetch = pltpu.make_async_copy(raw_hbm, raw_ref, load.at[0])
        keep = pltpu.make_async_copy(source_ref, kept_ref, load.at[1])
    else:
        fetch = pltpu.make_async_copy(kept_ref, source_ref, load.at[0])
    fetch.start()
    lower = lane_ids() < QUART
    rounds = SUB // batch
    steps = rounds * (sources // SUB)

    def forward(block):
        for w in range(windows):
            if bases[w] is None:
                x = [ins[w][RADIX + v * SUB : RADIX + (v + 1) * SUB, :] for v in range(RADIX)]
            else:
                spot = pl.ds(pl.multiple_of(bases[w] + block * SUB, SUB), SUB)
                x = [ins[w][spot, v * LANES : (v + 1) * LANES] for v in range(RADIX)]
            lift(x, twist_ref, grid_ref, w * PAD)
        grid_ref[...] = matmul(grid_ref[...], table_ref[...])
        for w in range(windows):
            re, im = whiten(grid_ref, w * PAD)
            for k in range(HALF):
                spec_ref[:, w * HALF + k, :LANES] = re[k]
                spec_ref[:, w * HALF + k, LANES:] = im[k]

    def place(step):
        block, within = lax.div(step, steps), lax.rem(step, steps)
        return block, lax.rem(within, rounds) * batch, pl.multiple_of(lax.div(within, rounds) * SUB, SUB)

    def copy(step, slot, c):
        block, start, group = place(step)
        target = out_ref.at[first + block * SUB + start + c, pl.ds(group, SUB), :]
        return pltpu.make_async_copy(page_ref.at[slot, c], target, sems.at[slot, c])

    def some(step, _):
        slot = lax.rem(step, 2)
        block, start, group = place(step)

        @pl.when(lax.rem(step, steps) == 0)
        def _():
            forward(block)

        if not fresh:
            pl.when(step == 0)(fetch.wait)

        @pl.when(step >= 2)
        def _():
            for c in range(batch):
                copy(step - 2, slot, c).wait()

        def combine(k):
            found = []
            parts = []
            for w in range(windows):
                spot = pl.ds(pl.multiple_of((w * HALF + k) * sources + group, SUB), SUB)
                parts.append((source_ref[spot, :LANES], source_ref[spot, LANES:]))
            for c in range(batch):
                re = im = None
                for w in range(windows):
                    ur, ui = parts[w]
                    row = w * HALF + k
                    sr = spec_ref[start + c, row : row + 1, :LANES]
                    si = spec_ref[start + c, row : row + 1, LANES:]
                    r, i = sr * ur + si * ui, si * ur - sr * ui
                    re, im = (r, i) if re is None else (re + r, im + i)
                found.append((re, im))
            return found

        for c, (re, im) in enumerate(combine(0)):
            cross_ref[pl.ds(c * PAD, SUB), :LANES] = jnp.where(lower, re, 0.0)
            cross_ref[pl.ds(c * PAD, SUB), LANES:] = jnp.where(lower, im, 0.0)
            cross_ref[pl.ds(c * PAD + HALF * SUB, SUB), :LANES] = jnp.where(lower, 0.0, re)
            cross_ref[pl.ds(c * PAD + HALF * SUB, SUB), LANES:] = jnp.where(lower, 0.0, im)
        for k in range(1, HALF):
            for c, (re, im) in enumerate(combine(k)):
                spot = pl.ds(c * PAD + k * SUB, SUB)
                cross_ref[spot, :LANES] = re
                cross_ref[spot, LANES:] = im
        cross_ref[...] = matmul(cross_ref[...], back_ref[...])
        for c in range(batch):
            re, im = [], []
            for k in range(ROWS):
                spot = pl.ds(c * PAD + k * SUB, SUB)
                r, i = cross_ref[spot, :LANES], cross_ref[spot, LANES:]
                if k == 0:
                    i = None
                else:
                    cos = twist_ref[k : k + 1, :]
                    sin = twist_ref[ROWS + k : ROWS + k + 1, :]
                    r, i = r * cos - i * sin, (None if k == HALF else i * cos + r * sin)
                re.append(r)
                im.append(i)
            lags = real_fft_adjoint(re, im)
            for v in range(RADIX):
                page_ref[slot, c, :, v * LANES : (v + 1) * LANES] = lags[v]
            copy(step, slot, c).start()
        return 0

    if fresh:
        fetch.wait()
        source_stage(windows, lax.axis_index("blk"), raw_ref, twist_ref, table_ref, weight_ref, source_ref, grid_ref)
        keep.start()
    every = steps * blocks
    lax.fori_loop(0, every, some, 0)
    for step in range(max(0, every - 2), every):
        for c in range(batch):
            copy(jnp.int32(step), step % 2, c).wait()
    if fresh:
        keep.wait()


def correlations(pieces, tables, total, first, rows, raw=None, source=None, before=None, batch=4):
    windows = len(pieces)
    sources = raw.shape[0] // (windows * RADIX) if source is None else source.shape[0] // (windows * HALF)
    args = [array for array, _ in pieces] + list(tables)
    inside, outside = pl.BlockSpec(memory_space=pltpu.VMEM), pl.BlockSpec(memory_space=pltpu.HBM)
    specs = [inside] * len(args)
    shapes = [jax.ShapeDtypeStruct((total, sources, NFFT), jnp.float32)]
    spectra = (windows * HALF * sources, 2 * LANES)
    scratch = [
        pltpu.VMEM(spectra, jnp.float32),
        pltpu.VMEM((windows * PAD, 2 * LANES), jnp.float32),
        pltpu.VMEM((SUB, windows * HALF, 2 * LANES), jnp.float32),
        pltpu.VMEM((batch * PAD, 2 * LANES), jnp.float32),
        pltpu.VMEM((2, batch, SUB, NFFT), jnp.float32),
        pltpu.SemaphoreType.DMA((2, batch)),
        pltpu.SemaphoreType.DMA((2,)),
    ]
    aliases = {}
    if source is None:
        args.append(raw)
        specs.append(outside)
        shapes.append(jax.ShapeDtypeStruct(spectra, jnp.float32))
        scratch.insert(5, pltpu.VMEM(raw.shape, jnp.float32))
    else:
        aliases = {len(args) + 1: 0}
        args += [source, before]
        specs += [outside, pl.BlockSpec(memory_space=pl.ANY)]
    return pl.pallas_call(
        functools.partial(main_kernel, windows, batch, first, rows // SUB, [base for _, base in pieces]),
        out_shape=shapes,
        in_specs=specs,
        out_specs=[outside] * len(shapes),
        scratch_shapes=scratch,
        input_output_aliases=aliases,
        compiler_params=pltpu.CompilerParams(vmem_limit_bytes=32 * 2**20),
        name=f"lags_{first}",
    )(*args)


def all_tables(norm):
    forward, back = dft_tables()
    return tuple(jnp.asarray(table) for table in (twist_table(), forward, back, bin_weights(norm)))


def live_window(gaps_ref):
    live, most = jnp.int32(0), gaps_ref[1, 0, 0]
    for slot in range(1, gaps_ref.shape[2]):
        better = gaps_ref[1, 0, slot] > most
        live = jnp.where(better, slot, live)
        most = jnp.where(better, gaps_ref[1, 0, slot], most)
    return live, gaps_ref[0, 0, live], most


def taper_kernel(mine, windows, lead, rest, gaps_hbm, taper_hbm, records_ref, *refs):
    outs, (gaps_ref, taper_ref, head_ref, load, sems) = refs[:-5], refs[-5:]
    here = lax.axis_index("tm")
    known = pltpu.make_async_copy(gaps_hbm, gaps_ref, load.at[0])
    shape = pltpu.make_async_copy(taper_hbm, taper_ref, load.at[1])
    known.start()
    shape.start()
    heads = [lax.rem(here + step, windows) * mine for step in lead] + [jnp.int32(0)] * bool(lead)
    copies = []
    for slot in range(gaps_ref.shape[2] if lead else 0):
        for n, base in enumerate(heads):
            spot = pl.ds(pl.multiple_of(base, SUB), SUB)
            source = records_ref.at[spot, pl.ds(slot * NFFT, NFFT)]
            copies.append(pltpu.make_async_copy(source, head_ref.at[slot, n], sems.at[len(copies)]))
    for copy in copies:
        copy.start()
    known.wait()
    live, start, most = live_window(gaps_ref)
    column = pl.ds(pl.multiple_of(live * NFFT, NFFT), NFFT)
    for n, (step, first, rows) in enumerate(rest):
        base = pl.multiple_of(lax.rem(here + step, windows) * mine + first, SUB)
        copies.append(pltpu.make_async_copy(records_ref.at[pl.ds(base, rows), column], outs[n], sems.at[n]))
        copies[-1].start()
    shape.wait()
    spots = lax.broadcasted_iota(jnp.int32, (1, NFFT), 1)
    taper = jnp.where((spots >= start) & (spots < start + most), taper_ref[...], 0.0)
    if lead:
        for copy in copies:
            copy.wait()
        line = jnp.where(spots == 0, live.astype(jnp.float32), head_ref[live, len(lead), :1, :] * taper)
        for v in range(RADIX):
            lanes = slice(v * LANES, (v + 1) * LANES)
            for n in range(len(lead)):
                outs[n][v : v + 1, :] = line[:, lanes]
                outs[n][RADIX + v * SUB : RADIX + (v + 1) * SUB, :] = head_ref[live, n, :, lanes] * taper[:, lanes]
            outs[len(lead)][v : v + 1, :] = line[:, lanes]
        return
    for n, copy in enumerate(copies):
        copy.wait()
        for r in range(0, outs[n].shape[0], SUB):
            outs[n][r : r + SUB, :] = outs[n][r : r + SUB, :] * taper


def tapered(records, gaps, mine, windows, lead, rest):
    spots = np.arange(NFFT)
    slots = gaps.shape[2]
    taper = jnp.asarray((0.5 - 0.5 * np.cos(2.0 * np.pi / NFFT * spots)).astype(np.float32)[None])
    shapes = [(RADIX * (1 + SUB), LANES)] * len(lead) + [(RADIX, LANES)] * bool(lead) + [(rows, NFFT) for _, _, rows in rest]
    args = [pltpu.with_memory_space_constraint(array, pltpu.HBM) for array in (gaps, taper, records)]
    return pl.pallas_call(
        functools.partial(taper_kernel, mine, windows, lead, rest),
        out_shape=[jax.ShapeDtypeStruct(shape, jnp.float32) for shape in shapes],
        in_specs=[pl.BlockSpec(memory_space=pltpu.HBM)] * 3,
        out_specs=[pl.BlockSpec(memory_space=pltpu.VMEM) for _ in shapes],
        scratch_shapes=[
            pltpu.SMEM(gaps.shape, jnp.int32),
            pltpu.VMEM(taper.shape, jnp.float32),
            pltpu.VMEM((slots, 1 + len(lead), SUB, NFFT), jnp.float32),
            pltpu.SemaphoreType.DMA((2,)),
            pltpu.SemaphoreType.DMA((max(len(rest), slots * (1 + len(lead))),)),
        ],
        compiler_params=pltpu.CompilerParams(vmem_limit_bytes=16 * 2**20),
        name="taper_lead" if lead else "taper",
    )(*args)


def shards(records, gaps):
    width = records.shape[0]
    slots = records.shape[1] // NFFT
    windows = lax.axis_size("tm")
    mine = width // windows
    cut = mine - SUB

    def shift(array, step):
        pairs = [(i, (i + step) % windows) for i in range(windows)]
        return lax.ppermute(array, "tm", pairs)

    steps = list(range(1, windows))
    order = sorted(steps, key=lambda d: (-min(d, windows - d), -d))
    *lead, row = tapered(records, gaps, mine, windows, steps, [])
    lead = dict(zip(steps, lead))
    lead = {d: shift(lead[d], d) for d in [order[0], order[1], order[2]]}
    rows = jnp.stack([row] + [lead[d][:RADIX] for d in steps])

    split = order
    first = [order[0], order[1], order[2]]
    rest = [(d, SUB, (cut if d in split else mine) - SUB) for d in first] + [(d, cut, SUB) for d in split] + [(0, 0, mine)]
    *bulk, own = tapered(records, gaps, mine, windows, [], rest)
    early, late = list(bulk[: len(steps)]), bulk[len(steps) :]
    rows, held = lax.optimization_barrier((rows, early[0]))
    early[0] = held
    raw = lax.all_gather(rows, "blk", axis=0, tiled=False)
    raw = raw.reshape(-1, LANES)
    early = {d: shift(array, d) for d, array in zip(first, early)}

    tables = all_tables(1.0 / math.sqrt(NFFT * slots * windows))
    pieces = [(own, 0)] + [(lead[d], None) for d in steps]
    more = [(own, SUB)] + [(early[d], 0) for d in steps]
    out, source = correlations(pieces, tables, mine, 0, SUB, raw=raw)
    source, late = lax.optimization_barrier((source, late))
    late = {d: shift(array, d) for d, array in zip(split, late)}
    (out,) = correlations(more, tables, mine, SUB, cut - SUB, source=source, before=out)
    pieces = [(own, cut)] + [(late[d], 0) if d in late else (early[d], cut - SUB) for d in steps]
    return correlations(pieces, tables, mine, cut, SUB, source=source, before=out)[0]


def solution(mesh):
    in_specs = (P("blk", "tm"), P(None, "blk", "tm"))
    out_specs = P(("blk", "tm"), None, None)
    return jax.shard_map(shards, mesh=mesh, in_specs=in_specs, out_specs=out_specs, check_vma=False)
```
